256 devices in a mesh: wide: 32 (over y, x, core), narrow: 8 (over z).
Axes of the slice: x: 4, y: 4, z: 8, core: 2. Of those that a mesh axis runs over, the one named last changes fastest.
Arguments:
- covariates: bfloat16 [524288, 128], P(('wide', 'narrow')), may hold values from -6 to 6
- level_codes: int32 [524288], P(('wide', 'narrow')), may hold values from 0 to 3
- sign_bits: int32 [524288], P(('wide', 'narrow')), may hold values from 0 to 1
- sample_rows: int32 [1024], P(('wide', 'narrow')), may hold values from 0 to 2047, as said below
- effects: float32 [512], replicated, may hold values from -6 to 6
- noise: float32 [524288], P(('wide', 'narrow')), may hold values from -8 to 8
Outputs:
- coefficients: float32 [512], replicated
- residual: float32 [524288], P(('wide', 'narrow'))
- factor: float32 [512, 512], replicated
The draws below stay inside these ranges and needn't reach their ends.
Inputs may be any that keep to these rules, and one draw needn't show every extreme that they name: `sample_rows`: a local row offset on the device that owns the entry.
All inputs are finite; a program needn't handle non-finite values.
Results may differ from the reference program's by a relative error of at most 0.0006.
The reference program's roundings to bfloat16 on the way count: a program that leaves them out, or rounds other values in their place, can miss the bound.
Values may be sent and summed in bfloat16 or wider, within the bound.
A program may use at most 64 MiB of HBM per device.

```python
import math
import jax
import jax.numpy as jnp
from jax import lax

COV = 128
LEVELS = 4
COLS = 512
ROWS_DEV = 2048
HB = 256
SKETCH = 1024
SAMP = 4
ITERS = 4
ROWS = 524288
N_WIDE = 32
N_NARROW = 8


def draw_sample_rows(key, part):
    key_values = jax.random.fold_in(key, 11)
    key_place = jax.random.fold_in(key, 12)
    key_other = jax.random.fold_in(key, 13)
    offsets = jax.random.randint(key_values, (SKETCH,), 0, ROWS_DEV, dtype=jnp.int32)
    top_place = jax.random.randint(key_place, (), 0, SKETCH, dtype=jnp.int32)
    step_other = jax.random.randint(key_other, (), 1, SKETCH, dtype=jnp.int32)
    low_place = (top_place + step_other) % SKETCH
    offsets = offsets.at[top_place].set(ROWS_DEV - 1)
    offsets = offsets.at[low_place].set(0)
    return offsets


def place_ends(array, own_key, smallest, high):
    dims = array.shape
    spot = [jax.random.randint(jax.random.fold_in(own_key, axis), (), 0, dims[axis]) for axis in range(len(dims))]
    array = array.at[tuple(spot)].set(smallest)
    longest = dims.index(max(dims))
    spot[longest] = (spot[longest] + 1) % dims[longest]
    return array.at[tuple(spot)].set(high)


def block_scale(rng, dims, split, least, largest):
    level, own = 1.0, jax.random.fold_in(rng, 6)
    for position, blocks in split:
        steps = jnp.exp(jax.random.uniform(jax.random.fold_in(own, position), (blocks,), jnp.float32, least / len(split), largest / len(split)))
        level = level * jnp.repeat(steps, dims[position] // blocks).reshape([-1 if axis == position else 1 for axis in range(len(dims))])
    return level


def bell_draw(own_key, shape, spread, most, pieces=(), kind=jnp.bfloat16):
    level = block_scale(own_key, shape, pieces, -0.22, 0.18) if pieces else 1.0
    array = jax.random.normal(own_key, shape, jnp.float32) * spread * level
    return jnp.minimum(jnp.maximum(array, -most), most).astype(kind)


def setup_inputs(seed: int = 0) -> dict:
    arg_keys = jax.random.split(jax.random.key(seed), 7)
    covariates = bell_draw(arg_keys[0], (ROWS, COV), 1.0, 6.0, ((0, 256),))
    level_codes = place_ends(jax.random.randint(arg_keys[1], (ROWS,), 0, LEVELS), jax.random.fold_in(arg_keys[1], 1), 0, LEVELS - 1).astype(jnp.int32)
    sign_bits = place_ends(jax.random.randint(arg_keys[2], (ROWS,), 0, 2), jax.random.fold_in(arg_keys[2], 1), 0, 1).astype(jnp.int32)
    sample_rows = draw_sample_rows(jax.random.fold_in(arg_keys[6], 71), 0)
    effects = bell_draw(arg_keys[4], (COLS,), 1.0, 6.0, (), jnp.float32)
    noise = bell_draw(arg_keys[5], (ROWS,), 3.0, 8.0, ((0, 256),), jnp.float32)
    return {"covariates": covariates, "level_codes": level_codes, "sign_bits": sign_bits, "sample_rows": sample_rows, "effects": effects, "noise": noise}


half_root = math.sqrt(0.5)

def hadamard(size):
    left = jnp.arange(size, dtype=jnp.int32)[:, None]
    right = jnp.arange(size, dtype=jnp.int32)[None, :]
    common = jnp.bitwise_and(left, right)
    parity = jnp.zeros((size, size), jnp.int32)
    for place in range(size.bit_length()):
        parity = parity + jnp.bitwise_and(jnp.right_shift(common, place), 1)
    return (1 - 2 * (parity % 2)).astype(jnp.float32)

def tri_solve(lower, vector, transpose):
    return lax.linalg.triangular_solve(lower, vector[:, None], left_side=True, lower=True, transpose_a=transpose)[:, 0]

def reference(covariates, level_codes, sign_bits, sample_rows, effects, noise):
    cols = LEVELS * COV
    table = hadamard(HB)
    cov_four = covariates.reshape(N_WIDE, N_NARROW, ROWS_DEV, COV).transpose(1, 0, 2, 3)
    code_three = level_codes.reshape(N_WIDE, N_NARROW, ROWS_DEV).transpose(1, 0, 2)
    sign_three = sign_bits.reshape(N_WIDE, N_NARROW, ROWS_DEV).transpose(1, 0, 2)
    samp_three = sample_rows.reshape(N_WIDE, N_NARROW, SAMP).transpose(1, 0, 2)

    def one_group(pack):
        cov_part, code_part, sign_part, samp_part = pack
        onehot = (code_part[..., None] == jnp.arange(LEVELS, dtype=jnp.int32)).astype(jnp.bfloat16)
        flipped = cov_part * (1 - 2 * sign_part).astype(jnp.bfloat16)[..., None]
        design = (onehot[..., None] * flipped[..., None, :]).reshape(N_WIDE, ROWS_DEV // HB, HB, cols)
        mixed = jnp.einsum('ij,wgjc->wgic', table, design.astype(jnp.float32), precision=lax.Precision.HIGHEST)
        mixed = (mixed * (1.0 / math.sqrt(HB))).astype(jnp.bfloat16).reshape(N_WIDE, ROWS_DEV, cols)
        for place in range(3):
            span = 2 ** place
            shaped = mixed.astype(jnp.float32).reshape(N_WIDE // (2 * span), 2, span, ROWS_DEV, cols)
            low = shaped[:, 0]
            high = shaped[:, 1]
            mixed = (jnp.stack([low + high, low - high], axis=1) * half_root).astype(jnp.bfloat16)
            mixed = mixed.reshape(N_WIDE, ROWS_DEV, cols)
        return jnp.take_along_axis(mixed, samp_part[:, :, None], axis=1)
    sketch = lax.map(one_group, (cov_four, code_three, sign_three, samp_three))
    sketch = sketch.transpose(1, 0, 2, 3).reshape(SKETCH, cols)
    gram = jnp.dot(sketch.T.astype(jnp.float32), sketch.astype(jnp.float32), preferred_element_type=jnp.float32)
    lower = jnp.linalg.cholesky(gram)
    factor = lower.T * math.sqrt(LEVELS / SKETCH)
    onehot = (level_codes[:, None] == jnp.arange(LEVELS, dtype=jnp.int32)[None, :]).astype(jnp.float32)
    wide_cov = covariates.astype(jnp.float32)

    def apply_design(vector):
        values = jnp.dot(wide_cov, vector.reshape(LEVELS, COV).T, precision=lax.Precision.HIGHEST)
        return lax.optimization_barrier(jnp.sum(values * onehot, axis=1))

    def adjoint(vector):
        return jnp.dot((onehot * vector[:, None]).T, wide_cov, precision=lax.Precision.HIGHEST).reshape(cols)
    timings = apply_design(effects) + noise
    resid = timings
    steer = tri_solve(lower, adjoint(resid), False)
    direction = steer
    gamma = jnp.sum(steer * steer)
    solved = jnp.zeros((cols,), jnp.float32)
    for step in range(ITERS):
        image = apply_design(tri_solve(lower, direction, True))
        alpha = gamma / jnp.sum(image * image)
        solved = solved + alpha * direction
        resid = resid - alpha * image
        steer = tri_solve(lower, adjoint(resid), False)
        gamma_new = jnp.sum(steer * steer)
        direction = steer + gamma_new / gamma * direction
        gamma = gamma_new
    return (tri_solve(lower, solved, True), resid, factor)
```

```python
import functools
import math

import jax
import jax.numpy as jnp
from jax import lax
from jax.experimental import pallas as pl
from jax.experimental.pallas import tpu as pltpu
from jax.sharding import PartitionSpec as P

COV = 128
LEVELS = 4
COLS = COV * LEVELS
ROWS = 2048
HB = 256
SKETCH = 1024
SAMP = 4
ITERS = 4
GROUP = 8
NZ = 8
NXY = 16
EXTRA = 8
LANES = 128

HALF_ROOT = math.sqrt(0.5)
HIGH = lax.Precision.HIGHEST
MESH = pl.DeviceIdType.MESH
F32 = jnp.float32
BF16 = jnp.bfloat16


def iota(shape, axis):
    return lax.broadcasted_iota(jnp.int32, shape, axis)


def split3(value):
    high = value.astype(BF16)
    rest = value - high.astype(F32)
    middle = rest.astype(BF16)
    low = (rest - middle.astype(F32)).astype(BF16)
    return high.astype(F32), middle.astype(F32), low.astype(F32)


def gather_kernel(
    samp_ref, cov_ref, codes_ref, bits_ref, noise_ref,
    sketch_ref, square_ref, extra_ref,
    own, asked, picks, lhs, sent, held, rowz,
    halves, half_in, pieces, piece_in, plane, plane_in,
    send, recv,
):
    wide = lax.axis_index("wide")
    z = lax.axis_index("narrow")
    core = lax.rem(wide, 2)
    q = wide // 2
    member = lax.rem(wide, GROUP)
    base = wide - member
    sibling = wide + 1 - 2 * core

    def mix_peer(o):
        return lax.rem(member + o, GROUP)

    def z_peer(o):
        return lax.rem(z + o, NZ)

    def xy_peer(o):
        return lax.rem(q + o, NXY)

    slots = iter(range(200))

    def remote(src, dst, to_wide, to_z):
        slot = next(slots)
        return pltpu.make_async_remote_copy(
            src_ref=src, dst_ref=dst, send_sem=send.at[slot], recv_sem=recv.at[slot],
            device_id=(to_wide, to_z), device_id_type=MESH,
        )

    barrier = pltpu.get_barrier_semaphore()
    greeted = 0
    for o in range(1, GROUP):
        pl.semaphore_signal(barrier, inc=1, device_id=(base + mix_peer(o), z), device_id_type=MESH)
        greeted += 1
    for o in range(1, NZ):
        pl.semaphore_signal(barrier, inc=1, device_id=(wide, z_peer(o)), device_id_type=MESH)
        greeted += 1
    for o in range(1, NXY):
        pl.semaphore_signal(
            barrier, inc=1, device_id=(2 * xy_peer(o) + core, z), device_id_type=MESH
        )
        greeted += 1

    for k in range(8):
        own[k : k + 1, :] = jnp.full((1, LANES), samp_ref[k % SAMP], jnp.int32)
    asked[member] = own[...]
    pl.semaphore_wait(barrier, greeted)

    ask = [remote(own, asked.at[member], base + mix_peer(o), z) for o in range(1, GROUP)]
    for copy in ask:
        copy.start()

    codes = codes_ref[...]
    flip = cov_ref[...].astype(F32).T
    for level in range(LEVELS):
        mask = (codes == level).astype(F32)
        lhs[level * COV : (level + 1) * COV, :] = (flip * mask).astype(BF16)
    masks = [(codes == level).astype(F32) for level in range(LEVELS)]
    parts = split3(noise_ref[...])
    shadow_rows = [part * mask for part in parts for mask in masks]
    shadow_rows = jnp.concatenate(shadow_rows + [jnp.zeros((4, ROWS), F32)], axis=0)
    normal = jnp.dot(lhs[...], cov_ref[...], preferred_element_type=F32)
    shadow = jnp.dot(shadow_rows.astype(BF16), cov_ref[...], preferred_element_type=F32)
    shadow = shadow[0:4] + shadow[4:8] + shadow[8:12]
    sub = iota((COV, COV), 0)
    lane = iota((COV, COV), 1)
    squares = []
    diagonals = []
    for pair in range(2):
        even = normal[2 * pair * COV : (2 * pair + 1) * COV]
        odd = normal[(2 * pair + 1) * COV : (2 * pair + 2) * COV]
        halves[pair, 0:COV, :] = jnp.where(lane >= sub, even, odd)
        diagonals.append(jnp.sum(jnp.where(lane == sub, odd, 0.0), axis=0, keepdims=True))
    extra = jnp.concatenate([shadow] + diagonals + [jnp.zeros((2, COV), F32)], axis=0)
    halves[0, COV:, :] = extra
    halves[1, COV:, :] = extra
    a_core = remote(halves.at[1 - core], half_in, sibling, z)
    a_core.start()

    for copy in ask:
        copy.wait_recv()
    want = jnp.concatenate([asked[i] for i in range(GROUP)], axis=0)
    shape = (GROUP * 8, LANES)
    common = want & iota(shape, 1)
    common = common ^ (common >> 4)
    common = common ^ (common >> 2)
    low = common ^ (common >> 1)
    top = (want >> 7) & 1
    block = want >> 8
    for chunk in range(ROWS // LANES):
        span = slice(chunk * LANES, (chunk + 1) * LANES)
        parity = low ^ bits_ref[:, span]
        if chunk % 2:
            parity = parity ^ top
        sign = (1 - 2 * (parity & 1)).astype(F32)
        sign = jnp.where(block == chunk // 2, sign, 0.0)
        here = codes_ref[:, span]
        for level in range(LEVELS):
            value = sign * (here == level).astype(F32)
            picks[level * 64 : (level + 1) * 64, span] = value.astype(BF16)
    local = jnp.dot(picks[...], cov_ref[...], preferred_element_type=F32)
    local = local * (1.0 / math.sqrt(HB))
    local = jnp.concatenate([local[level * 64 : (level + 1) * 64] for level in range(LEVELS)], axis=1)
    for i in range(GROUP):
        sent[i] = local[i * 8 : i * 8 + SAMP].astype(BF16)
    held[member] = sent[member]
    rows = [
        remote(sent.at[mix_peer(o)], held.at[member], base + mix_peer(o), z)
        for o in range(1, GROUP)
    ]
    for copy in rows:
        copy.start()

    a_core.wait_recv()
    mine = halves[core] + half_in[...]
    for i in range(NZ):
        pieces[i] = jnp.concatenate([mine[i * 16 : (i + 1) * 16], mine[COV:]], axis=0)
    piece_in[z] = pieces[z]
    a_z = [
        remote(pieces.at[z_peer(o)], piece_in.at[z], wide, z_peer(o)) for o in range(1, NZ)
    ]

    for copy in rows:
        copy.wait_recv()
    level_rows = [held[i].astype(F32) for i in range(GROUP)]
    for place in range(3):
        side = (1 - 2 * lax.rem(wide // (2**place), 2)).astype(F32)
        level_rows = [
            ((level_rows[i] + side * level_rows[i + 1]) * HALF_ROOT).astype(BF16).astype(F32)
            for i in range(0, len(level_rows), 2)
        ]
    rowz[z] = level_rows[0].astype(BF16)
    s_z = [remote(rowz.at[z], rowz.at[z], wide, z_peer(o)) for o in range(1, NZ)]
    for copy in s_z:
        copy.start()
    for copy in a_z:
        copy.start()

    for copy in s_z:
        copy.wait_recv()
    stack = jnp.concatenate([rowz[i].astype(F32) for i in range(NZ)], axis=0)
    sketch_ref[core, q] = stack.astype(BF16)
    s_xy = [
        remote(sketch_ref.at[core, q], sketch_ref.at[core, q], 2 * xy_peer(o) + core, z)
        for o in range(1, NXY)
    ]
    for copy in s_xy:
        copy.start()
    s_core = [remote(sketch_ref.at[core, q], sketch_ref.at[core, q], sibling, z)]
    s_core[0].start()

    for copy in a_z:
        copy.wait_recv()
    total = piece_in[0]
    for i in range(1, NZ):
        total = total + piece_in[i]
    plane_in[q] = total
    a_xy = [
        remote(plane_in.at[q], plane_in.at[q], 2 * xy_peer(o) + core, z) for o in range(1, NXY)
    ]
    for copy in a_xy:
        copy.start()

    for o in range(1, NXY):
        s_xy[o - 1].wait_recv()
        from_q = lax.rem(q - o + NXY, NXY)
        copy = remote(sketch_ref.at[core, from_q], sketch_ref.at[core, from_q], sibling, z)
        copy.start()
        s_core.append(copy)

    for copy in a_xy:
        copy.wait_recv()
    total = plane_in[0]
    for i in range(1, NXY):
        total = total + plane_in[i]
    extra_ref[...] = total[16:]
    square_ref[core, z] = total[:16]
    a_out = [
        remote(square_ref.at[core, z], square_ref.at[core, z], wide, z_peer(o))
        for o in range(1, NZ)
    ]
    for copy in a_out:
        copy.start()
    for copy in a_out:
        copy.wait_recv()
    a_last = remote(square_ref.at[core], square_ref.at[core], sibling, z)
    a_last.start()
    a_last.wait_recv()
    for copy in s_core:
        copy.wait_recv()
    for copy in ask + [a_core] + rows + a_z + s_z + s_xy + a_xy + s_core + a_out + [a_last]:
        copy.wait_send()


N_COPIES = 3 * 7 + 1 + 7 + 1 + 15 + 15 + 15 + 7 + 1


def gather(samples, covariates, codes, bits, noise):
    vmem = pl.BlockSpec(memory_space=pltpu.VMEM)
    smem = pl.BlockSpec(memory_space=pltpu.SMEM)
    return pl.pallas_call(
        gather_kernel,
        out_shape=(
            jax.ShapeDtypeStruct((2, NXY, 32, COLS), BF16),
            jax.ShapeDtypeStruct((2, NZ, 16, COV), F32),
            jax.ShapeDtypeStruct((EXTRA, COV), F32),
        ),
        in_specs=[smem, vmem, vmem, vmem, vmem],
        out_specs=(vmem, vmem, vmem),
        scratch_shapes=[
            pltpu.VMEM((8, LANES), jnp.int32),
            pltpu.VMEM((GROUP, 8, LANES), jnp.int32),
            pltpu.VMEM((LEVELS * 64, ROWS), BF16),
            pltpu.VMEM((COLS, ROWS), BF16),
            pltpu.VMEM((GROUP, SAMP, COLS), BF16),
            pltpu.VMEM((GROUP, SAMP, COLS), BF16),
            pltpu.VMEM((NZ, SAMP, COLS), BF16),
            pltpu.VMEM((2, COV + EXTRA, COV), F32),
            pltpu.VMEM((COV + EXTRA, COV), F32),
            pltpu.VMEM((NZ, 16 + EXTRA, COV), F32),
            pltpu.VMEM((NZ, 16 + EXTRA, COV), F32),
            pltpu.VMEM((16 + EXTRA, COV), F32),
            pltpu.VMEM((NXY, 16 + EXTRA, COV), F32),
            pltpu.SemaphoreType.DMA((N_COPIES,)),
            pltpu.SemaphoreType.DMA((N_COPIES,)),
        ],
        compiler_params=pltpu.CompilerParams(
            collective_id=0, has_side_effects=True, vmem_limit_bytes=40 << 20
        ),
        name="gather_sketch",
    )(samples, covariates, codes, bits, noise)


def spread(value, index):
    return jnp.broadcast_to(value[index : index + 1, :], value.shape)


def invert_factor(matrix):
    count = COV // 8
    rows = [matrix[8 * t : 8 * t + 8, :] for t in range(count)]
    sub = iota((8, COV), 0)
    lane = iota((8, COV), 1)
    for p in range(count):
        first = 8 * p
        own = [
            [jnp.broadcast_to(rows[t][:, first + i : first + i + 1], (8, COV)) for t in range(p, count)]
            for i in range(8)
        ]
        panel = (lane >= first) & (lane < first + 8)
        for t in range(p + 1, count):
            rows[t] = jnp.where(panel, 0.0, rows[t])
        rows[p] = jnp.where(panel, jnp.where(lane == first + sub, 1.0, 0.0), rows[p])
        for i in range(8):
            root = lax.rsqrt(spread(own[i][0], i))
            row = spread(rows[p], i) * root
            upper = {k: spread(own[k][0], i) * root for k in range(i + 1, 8)}
            for t in range(p, count):
                scale = own[i][t - p] * root
                if t == p:
                    scale = jnp.where(sub > i, scale, 0.0)
                    rows[t] = jnp.where(sub == i, row, rows[t] - scale * row)
                else:
                    rows[t] = rows[t] - scale * row
                for k in range(i + 1, 8):
                    own[k][t - p] = own[k][t - p] - scale * upper[k]
    for p in range(count):
        rows[p] = jnp.where(lane <= 8 * p + sub, rows[p], 0.0)
    return jnp.concatenate(rows, axis=0)


def blk(index):
    return slice(index * COV, (index + 1) * COV)


def solve_kernel(
    sketch_ref, square_ref, extra_ref, effects_ref, cov_ref, codes_ref, noise_ref,
    coef_ref, resid_ref, factor_ref, gram, inverse,
):
    n = LEVELS
    sub = iota((COV, COV), 0)
    lane = iota((COV, COV), 1)
    scale = math.sqrt(LEVELS / SKETCH)
    for k in range(n):
        gram[k, :, k * COV :] = lax.dot_general(
            sketch_ref[:, blk(k)], sketch_ref[:, k * COV :], (((0,), (0,)), ((), ())),
            preferred_element_type=F32,
        )
    for k in range(n):
        corner = invert_factor(gram[k, :, blk(k)])
        inverse[k, :, blk(k)] = corner
        product = jnp.dot(corner, gram[k], precision=HIGH, preferred_element_type=F32)
        if k:
            inverse[k, :, : k * COV] = product[:, : k * COV]
            factor_ref[blk(k), : k * COV] = jnp.zeros((COV, k * COV), F32)
        factor_ref[blk(k), blk(k)] = jnp.where(lane >= sub, product[:, blk(k)], 0.0) * scale
        if k + 1 < n:
            factor_ref[blk(k), (k + 1) * COV :] = product[:, (k + 1) * COV :] * scale
        for i in range(k + 1, n):
            back = product[:, blk(i)].T
            change = jnp.dot(back, product[:, i * COV :], precision=HIGH, preferred_element_type=F32)
            gram[i, :, i * COV :] = gram[i, :, i * COV :] - change
        for i in range(k + 1, n):
            back = product[:, blk(i)].T
            gram[i, :, blk(k)] = -jnp.dot(back, corner, precision=HIGH, preferred_element_type=F32)
            if k:
                change = jnp.dot(back, product[:, : k * COV], precision=HIGH, preferred_element_type=F32)
                gram[i, :, : k * COV] = gram[i, :, : k * COV] - change

    normal = []
    for pair in range(2):
        square = square_ref[pair]
        turned = square.T
        diagonal = extra_ref[4 + pair : 5 + pair, :]
        normal.append(jnp.where(lane >= sub, square, turned))
        normal.append(jnp.where(lane < sub, square, jnp.where(lane > sub, turned, diagonal)))

    def apply_normal(rows):
        out = []
        for level in range(n):
            column = jnp.sum(normal[level] * rows[level], axis=1, keepdims=True)
            out.append(jnp.sum(jnp.where(lane == sub, column, 0.0), axis=0, keepdims=True))
        return out

    def forward(rows):
        out = []
        for k in range(n):
            acc = inverse[k, :, blk(0)] * rows[0]
            for c in range(1, k + 1):
                acc = acc + inverse[k, :, blk(c)] * rows[c]
            out.append(jnp.sum(acc, axis=1, keepdims=True))
        return out

    def backward(columns):
        out = []
        for c in range(n):
            acc = inverse[c, :, blk(c)] * columns[c]
            for k in range(c + 1, n):
                acc = acc + inverse[k, :, blk(c)] * columns[k]
            out.append(jnp.sum(acc, axis=0, keepdims=True))
        return out

    def dot(left, right, axis):
        acc = left[0] * right[0]
        for a, b in zip(left[1:], right[1:]):
            acc = acc + a * b
        return jnp.sum(acc, axis=axis, keepdims=True)

    effects = [effects_ref[:, blk(level)] for level in range(n)]
    gradient = [
        image + extra_ref[level : level + 1, :] for level, image in enumerate(apply_normal(effects))
    ]
    steer = forward(gradient)
    gamma = dot(steer, steer, 0)
    direction = backward(steer)
    solved = [jnp.zeros((1, COV), F32)] * n
    for step in range(ITERS):
        image = apply_normal(direction)
        alpha = gamma / dot(direction, image, 1)
        solved = [a + alpha * b for a, b in zip(solved, direction)]
        if step + 1 < ITERS:
            gradient = [a - alpha * b for a, b in zip(gradient, image)]
            steer = forward(gradient)
            gamma_new = dot(steer, steer, 0)
            ratio = gamma_new / gamma
            direction = [a + ratio * b for a, b in zip(backward(steer), direction)]
            gamma = gamma_new
    left = []
    for level in range(n):
        coef_ref[:, blk(level)] = solved[level]
        left.append(effects[level] - solved[level])
    parts = split3(jnp.concatenate(left, axis=0))
    weights = jnp.concatenate(list(parts) + [jnp.zeros((4, COV), F32)], axis=0).astype(BF16)
    values = lax.dot_general(
        weights, cov_ref[...], (((1,), (1,)), ((), ())), preferred_element_type=F32
    )
    codes = codes_ref[...]
    resid = noise_ref[...]
    for level in range(n):
        value = values[level : level + 1] + values[4 + level : 5 + level] + values[8 + level : 9 + level]
        resid = resid + jnp.where(codes == level, value, 0.0)
    resid_ref[...] = resid


def solve(sketch, square, extra, effects, covariates, codes, noise):
    vmem = pl.BlockSpec(memory_space=pltpu.VMEM)
    return pl.pallas_call(
        solve_kernel,
        out_shape=(
            jax.ShapeDtypeStruct((1, COLS), F32),
            jax.ShapeDtypeStruct((1, ROWS), F32),
            jax.ShapeDtypeStruct((COLS, COLS), F32),
        ),
        in_specs=[vmem] * 7,
        out_specs=(vmem,) * 3,
        scratch_shapes=[
            pltpu.VMEM((LEVELS, COV, COLS), F32),
            pltpu.VMEM((LEVELS, COV, COLS), F32),
        ],
        compiler_params=pltpu.CompilerParams(vmem_limit_bytes=40 << 20),
        name="solve",
    )(sketch, square, extra, effects, covariates, codes, noise)


def body(covariates, level_codes, sign_bits, sample_rows, effects, noise):
    codes = level_codes.reshape(1, ROWS)
    noise = noise.reshape(1, ROWS)
    sketch, square, extra = gather(
        sample_rows, covariates, codes, sign_bits.reshape(1, ROWS), noise
    )
    coef, resid, factor = solve(
        sketch.reshape(SKETCH, COLS), square.reshape(2, COV, COV), extra,
        effects.reshape(1, COLS), covariates, codes, noise,
    )
    return coef.reshape(COLS), resid.reshape(ROWS), factor


def solution(mesh):
    rows = P(("wide", "narrow"))
    return jax.shard_map(
        body,
        mesh=mesh,
        in_specs=(P(("wide", "narrow"), None), rows, rows, rows, P(), rows),
        out_specs=(P(), rows, P()),
        check_vma=False,
    )
```

```python
import functools
import math

import jax
import jax.numpy as jnp
from jax import lax
from jax.experimental import pallas as pl
from jax.experimental.pallas import tpu as pltpu
from jax.sharding import PartitionSpec as P

COV = 128
LEVELS = 4
COLS = COV * LEVELS
ROWS = 2048
HB = 256
SKETCH = 1024
SAMP = 4
ITERS = 4
GROUP = 8
NZ = 8
NXY = 16
EXTRA = 8
LANES = 128

HALF_ROOT = math.sqrt(0.5)
HIGH = lax.Precision.HIGHEST
MESH = pl.DeviceIdType.MESH
F32 = jnp.float32
BF16 = jnp.bfloat16


def iota(shape, axis):
    return lax.broadcasted_iota(jnp.int32, shape, axis)


def split3(value):
    high = value.astype(BF16)
    rest = value - high.astype(F32)
    middle = rest.astype(BF16)
    low = (rest - middle.astype(F32)).astype(BF16)
    return high.astype(F32), middle.astype(F32), low.astype(F32)


def ring(offset, size):
    return min(offset, size - offset)


Z_FAR = sorted(range(1, NZ), key=lambda o: -ring(o, NZ))
XY_FAR = sorted(
    [(dy, dx) for dy in range(4) for dx in range(4) if (dy, dx) != (0, 0)],
    key=lambda o: -(ring(o[0], 4) + ring(o[1], 4)),
)
MIX_FAR = sorted(
    [(dx, dc) for dx in range(4) for dc in range(2) if (dx, dc) != (0, 0)],
    key=lambda o: -(ring(o[0], 4) + o[1]),
)


def gather_kernel(
    samp_hbm, cov_hbm, codes_hbm, bits_hbm, noise_hbm,
    sketch_ref, square_ref, extra_ref,
    samp_ref, cov_ref, codes_ref, bits_ref, noise_ref,
    own, asked, picks, lhs, sent, held, rowz,
    halves, half_in, pieces, piece_in, plane_in,
    send, recv, load,
):
    loads = [
        pltpu.make_async_copy(src, dst, load.at[i])
        for i, (src, dst) in enumerate(
            [
                (samp_hbm, samp_ref), (cov_hbm, cov_ref), (codes_hbm, codes_ref),
                (bits_hbm, bits_ref), (noise_hbm, noise_ref),
            ]
        )
    ]
    for copy in loads:
        copy.start()
    wide = lax.axis_index("wide")
    z = lax.axis_index("narrow")
    core = lax.rem(wide, 2)
    q = wide // 2
    x = lax.rem(q, 4)
    y = q // 4
    member = lax.rem(wide, GROUP)
    base = wide - member
    sibling = wide + 1 - 2 * core
    mix_peers = [lax.rem(x + dx, 4) * 2 + lax.rem(core + dc, 2) for dx, dc in MIX_FAR]
    z_peers = [lax.rem(z + o, NZ) for o in Z_FAR]
    xy_peers = [lax.rem(y + dy, 4) * 4 + lax.rem(x + dx, 4) for dy, dx in XY_FAR]

    slots = iter(range(N_COPIES))

    def remote(src, dst, to_wide, to_z):
        slot = next(slots)
        return pltpu.make_async_remote_copy(
            src_ref=src, dst_ref=dst, send_sem=send.at[slot], recv_sem=recv.at[slot],
            device_id=(to_wide, to_z), device_id_type=MESH,
        )

    barrier = pltpu.get_barrier_semaphore()
    for peer in z_peers:
        pl.semaphore_signal(barrier, inc=1, device_id=(wide, peer), device_id_type=MESH)
    for peer in xy_peers:
        pl.semaphore_signal(barrier, inc=1, device_id=(2 * peer + core, z), device_id_type=MESH)
    for peer in mix_peers:
        pl.semaphore_signal(barrier, inc=1, device_id=(base + peer, z), device_id_type=MESH)

    loads[0].wait()
    for k in range(8):
        own[k : k + 1, :] = jnp.full((1, LANES), samp_ref[k % SAMP], jnp.int32)
    asked[member] = own[...]
    pl.semaphore_wait(barrier, len(Z_FAR) + len(XY_FAR) + len(MIX_FAR))

    ask = [remote(own, asked.at[member], base + peer, z) for peer in mix_peers]
    for copy in ask:
        copy.start()

    for copy in loads[1:]:
        copy.wait()
    codes = codes_ref[...]
    flip = cov_ref[...].astype(F32).T
    masks = [(codes == level).astype(F32) for level in range(LEVELS)]
    for level in range(LEVELS):
        lhs[level * COV : (level + 1) * COV, :] = (flip * masks[level]).astype(BF16)
    parts = split3(noise_ref[...])
    shadow_rows = [part * mask for part in parts for mask in masks]
    shadow_rows = jnp.concatenate(shadow_rows + [jnp.zeros((4, ROWS), F32)], axis=0)
    normal = jnp.dot(lhs[...], cov_ref[...], preferred_element_type=F32)
    shadow = jnp.dot(shadow_rows.astype(BF16), cov_ref[...], preferred_element_type=F32)
    shadow = shadow[0:4] + shadow[4:8] + shadow[8:12]
    sub = iota((COV, COV), 0)
    lane = iota((COV, COV), 1)
    diagonals = []
    for pair in range(2):
        even = normal[2 * pair * COV : (2 * pair + 1) * COV]
        odd = normal[(2 * pair + 1) * COV : (2 * pair + 2) * COV]
        halves[pair, 0:COV, :] = jnp.where(lane >= sub, even, odd)
        diagonals.append(jnp.sum(jnp.where(lane == sub, odd, 0.0), axis=0, keepdims=True))
    extra = jnp.concatenate([shadow] + diagonals + [jnp.zeros((2, COV), F32)], axis=0)
    halves[0, COV:, :] = extra
    halves[1, COV:, :] = extra
    a_core = remote(halves.at[1 - core], half_in, sibling, z)
    a_core.start()

    for copy in ask:
        copy.wait_recv()
    want = jnp.concatenate([asked[i] for i in range(GROUP)], axis=0)
    shape = (GROUP * 8, LANES)
    common = want & iota(shape, 1)
    common = common ^ (common >> 4)
    common = common ^ (common >> 2)
    low = common ^ (common >> 1)
    top = (want >> 7) & 1
    block = want >> 8
    for chunk in range(ROWS // LANES):
        span = slice(chunk * LANES, (chunk + 1) * LANES)
        parity = low ^ bits_ref[:, span]
        if chunk % 2:
            parity = parity ^ top
        sign = (1 - 2 * (parity & 1)).astype(F32)
        sign = jnp.where(block == chunk // 2, sign, 0.0)
        here = codes_ref[:, span]
        for level in range(LEVELS):
            value = sign * (here == level).astype(F32)
            picks[level * 64 : (level + 1) * 64, span] = value.astype(BF16)
    local = jnp.dot(picks[...], cov_ref[...], preferred_element_type=F32)
    local = local * (1.0 / math.sqrt(HB))
    local = jnp.concatenate([local[level * 64 : (level + 1) * 64] for level in range(LEVELS)], axis=1)
    for i in range(GROUP):
        sent[i] = local[i * 8 : i * 8 + SAMP].astype(BF16)
    held[member] = sent[member]
    rows = [remote(sent.at[peer], held.at[member], base + peer, z) for peer in mix_peers]
    for copy in rows:
        copy.start()

    a_core.wait_recv()
    mine = halves[core] + half_in[...]
    for i in range(NZ):
        pieces[i] = jnp.concatenate([mine[i * 16 : (i + 1) * 16], mine[COV:]], axis=0)
    piece_in[z] = pieces[z]
    a_z = [remote(pieces.at[peer], piece_in.at[z], wide, peer) for peer in z_peers]
    for copy in a_z:
        copy.start()

    for copy in rows:
        copy.wait_recv()
    level_rows = [held[i].astype(F32) for i in range(GROUP)]
    for place in range(3):
        side = (1 - 2 * lax.rem(wide // (2**place), 2)).astype(F32)
        level_rows = [
            ((level_rows[i] + side * level_rows[i + 1]) * HALF_ROOT).astype(BF16).astype(F32)
            for i in range(0, len(level_rows), 2)
        ]
    rowz[z] = level_rows[0].astype(BF16)
    s_z = [remote(rowz.at[z], rowz.at[z], wide, peer) for peer in z_peers]
    for copy in s_z:
        copy.start()

    for copy in a_z:
        copy.wait_recv()
    total = piece_in[0]
    for i in range(1, NZ):
        total = total + piece_in[i]
    plane_in[q] = total
    a_xy = [remote(plane_in.at[q], plane_in.at[q], 2 * peer + core, z) for peer in xy_peers]
    for copy in a_xy:
        copy.start()

    for copy in s_z:
        copy.wait_recv()
    stack = jnp.concatenate([rowz[i].astype(F32) for i in range(NZ)], axis=0)
    block = sketch_ref.at[core, q]
    block[...] = stack.astype(BF16)
    s_xy = [remote(block, block, 2 * peer + core, z) for peer in xy_peers]
    for copy in s_xy:
        copy.start()
    s_core = [remote(block, block, sibling, z)]
    s_core[0].start()

    for copy in a_xy:
        copy.wait_recv()
    total = plane_in[0]
    for i in range(1, NXY):
        total = total + plane_in[i]
    extra_ref[...] = total[16:]
    square_ref[core, z] = total[:16]
    mine = square_ref.at[core, z]
    a_out = [remote(mine, mine, wide, peer) for peer in z_peers]
    for copy in a_out:
        copy.start()

    def onward(index):
        dy, dx = XY_FAR[index]
        s_xy[index].wait_recv()
        from_q = lax.rem(y - dy + 4, 4) * 4 + lax.rem(x - dx + 4, 4)
        passed = sketch_ref.at[core, from_q]
        copy = remote(passed, passed, sibling, z)
        copy.start()
        s_core.append(copy)

    nearest = list(range(len(XY_FAR)))[::-1]
    for index in nearest[:10]:
        onward(index)
    for copy in a_out:
        copy.wait_recv()
    a_last = remote(square_ref.at[core], square_ref.at[core], sibling, z)
    a_last.start()
    for index in nearest[10:]:
        onward(index)
    a_last.wait_recv()
    for copy in s_core:
        copy.wait_recv()
    for copy in ask + [a_core] + rows + a_z + s_z + s_xy + a_xy + s_core + a_out + [a_last]:
        copy.wait_send()


N_COPIES = 3 * 7 + 1 + 7 + 1 + 15 + 15 + 15 + 7 + 1


def gather(samples, covariates, codes, bits, noise):
    vmem = pl.BlockSpec(memory_space=pltpu.VMEM)
    hbm = pl.BlockSpec(memory_space=pltpu.HBM)
    return pl.pallas_call(
        gather_kernel,
        out_shape=(
            jax.ShapeDtypeStruct((2, NXY, 32, COLS), BF16),
            jax.ShapeDtypeStruct((2, NZ, 16, COV), F32),
            jax.ShapeDtypeStruct((EXTRA, COV), F32),
        ),
        in_specs=[hbm] * 5,
        out_specs=(vmem, vmem, vmem),
        scratch_shapes=[
            pltpu.SMEM((SAMP,), jnp.int32),
            pltpu.VMEM((ROWS, COV), BF16),
            pltpu.VMEM((1, ROWS), jnp.int32),
            pltpu.VMEM((1, ROWS), jnp.int32),
            pltpu.VMEM((1, ROWS), F32),
            pltpu.VMEM((8, LANES), jnp.int32),
            pltpu.VMEM((GROUP, 8, LANES), jnp.int32),
            pltpu.VMEM((LEVELS * 64, ROWS), BF16),
            pltpu.VMEM((COLS, ROWS), BF16),
            pltpu.VMEM((GROUP, SAMP, COLS), BF16),
            pltpu.VMEM((GROUP, SAMP, COLS), BF16),
            pltpu.VMEM((NZ, SAMP, COLS), BF16),
            pltpu.VMEM((2, COV + EXTRA, COV), F32),
            pltpu.VMEM((COV + EXTRA, COV), F32),
            pltpu.VMEM((NZ, 16 + EXTRA, COV), F32),
            pltpu.VMEM((NZ, 16 + EXTRA, COV), F32),
            pltpu.VMEM((NXY, 16 + EXTRA, COV), F32),
            pltpu.SemaphoreType.DMA((N_COPIES,)),
            pltpu.SemaphoreType.DMA((N_COPIES,)),
            pltpu.SemaphoreType.DMA((5,)),
        ],
        compiler_params=pltpu.CompilerParams(
            collective_id=0, has_side_effects=True, vmem_limit_bytes=40 << 20
        ),
        name="gather_sketch",
    )(samples, covariates, codes, bits, noise)


def spread(value, index):
    return jnp.broadcast_to(value[index : index + 1, :], value.shape)


def invert_factor(matrix):
    count = COV // 8
    rows = [matrix[8 * t : 8 * t + 8, :] for t in range(count)]
    sub = iota((8, COV), 0)
    lane = iota((8, COV), 1)
    for p in range(count):
        first = 8 * p
        own = [
            [jnp.broadcast_to(rows[t][:, first + i : first + i + 1], (8, COV)) for t in range(p, count)]
            for i in range(8)
        ]
        panel = (lane >= first) & (lane < first + 8)
        for t in range(p + 1, count):
            rows[t] = jnp.where(panel, 0.0, rows[t])
        rows[p] = jnp.where(panel, jnp.where(lane == first + sub, 1.0, 0.0), rows[p])
        for i in range(8):
            root = lax.rsqrt(spread(own[i][0], i))
            row = spread(rows[p], i) * root
            upper = {k: spread(own[k][0], i) * root for k in range(i + 1, 8)}
            for t in range(p, count):
                scale = own[i][t - p] * root
                if t == p:
                    scale = jnp.where(sub > i, scale, 0.0)
                    rows[t] = jnp.where(sub == i, row, rows[t] - scale * row)
                else:
                    rows[t] = rows[t] - scale * row
                for k in range(i + 1, 8):
                    own[k][t - p] = own[k][t - p] - scale * upper[k]
    for p in range(count):
        rows[p] = jnp.where(lane <= 8 * p + sub, rows[p], 0.0)
    return jnp.concatenate(rows, axis=0)


def blk(index):
    return slice(index * COV, (index + 1) * COV)


def solve_kernel(
    sketch_ref, square_ref, extra_ref, effects_hbm, cov_hbm, codes_hbm, noise_hbm,
    coef_ref, resid_ref, factor_hbm, gram, inverse,
    factor_ref, effects_ref, cov_ref, codes_ref, noise_ref, load, store,
):
    loads = [
        pltpu.make_async_copy(src, dst, load.at[i])
        for i, (src, dst) in enumerate(
            [
                (effects_hbm, effects_ref), (cov_hbm, cov_ref), (codes_hbm, codes_ref),
                (noise_hbm, noise_ref),
            ]
        )
    ]
    for copy in loads:
        copy.start()
    stores = []
    n = LEVELS
    sub = iota((COV, COV), 0)
    lane = iota((COV, COV), 1)
    scale = math.sqrt(LEVELS / SKETCH)
    for k in range(n):
        gram[k, :, k * COV :] = lax.dot_general(
            sketch_ref[:, blk(k)], sketch_ref[:, k * COV :], (((0,), (0,)), ((), ())),
            preferred_element_type=F32,
        )
    for k in range(n):
        corner = invert_factor(gram[k, :, blk(k)])
        inverse[k, :, blk(k)] = corner
        product = jnp.dot(corner, gram[k], precision=HIGH, preferred_element_type=F32)
        if k:
            inverse[k, :, : k * COV] = product[:, : k * COV]
            factor_ref[blk(k), : k * COV] = jnp.zeros((COV, k * COV), F32)
        factor_ref[blk(k), blk(k)] = jnp.where(lane >= sub, product[:, blk(k)], 0.0) * scale
        if k + 1 < n:
            factor_ref[blk(k), (k + 1) * COV :] = product[:, (k + 1) * COV :] * scale
        part = pltpu.make_async_copy(factor_ref.at[blk(k)], factor_hbm.at[blk(k)], store.at[k])
        part.start()
        stores.append(part)
        for i in range(k + 1, n):
            back = product[:, blk(i)].T
            change = jnp.dot(back, product[:, i * COV :], precision=HIGH, preferred_element_type=F32)
            gram[i, :, i * COV :] = gram[i, :, i * COV :] - change
        for i in range(k + 1, n):
            back = product[:, blk(i)].T
            gram[i, :, blk(k)] = -jnp.dot(back, corner, precision=HIGH, preferred_element_type=F32)
            if k:
                change = jnp.dot(back, product[:, : k * COV], precision=HIGH, preferred_element_type=F32)
                gram[i, :, : k * COV] = gram[i, :, : k * COV] - change

    normal = []
    for pair in range(2):
        square = square_ref[pair]
        turned = square.T
        diagonal = extra_ref[4 + pair : 5 + pair, :]
        normal.append(jnp.where(lane >= sub, square, turned))
        normal.append(jnp.where(lane < sub, square, jnp.where(lane > sub, turned, diagonal)))

    def apply_normal(rows):
        out = []
        for level in range(n):
            column = jnp.sum(normal[level] * rows[level], axis=1, keepdims=True)
            out.append(jnp.sum(jnp.where(lane == sub, column, 0.0), axis=0, keepdims=True))
        return out

    def forward(rows):
        out = []
        for k in range(n):
            acc = inverse[k, :, blk(0)] * rows[0]
            for c in range(1, k + 1):
                acc = acc + inverse[k, :, blk(c)] * rows[c]
            out.append(jnp.sum(acc, axis=1, keepdims=True))
        return out

    def backward(columns):
        out = []
        for c in range(n):
            acc = inverse[c, :, blk(c)] * columns[c]
            for k in range(c + 1, n):
                acc = acc + inverse[k, :, blk(c)] * columns[k]
            out.append(jnp.sum(acc, axis=0, keepdims=True))
        return out

    def dot(left, right, axis):
        acc = left[0] * right[0]
        for a, b in zip(left[1:], right[1:]):
            acc = acc + a * b
        return jnp.sum(acc, axis=axis, keepdims=True)

    for copy in loads:
        copy.wait()
    effects = [effects_ref[:, blk(level)] for level in range(n)]
    gradient = [
        image + extra_ref[level : level + 1, :] for level, image in enumerate(apply_normal(effects))
    ]
    steer = forward(gradient)
    gamma = dot(steer, steer, 0)
    direction = backward(steer)
    solved = [jnp.zeros((1, COV), F32)] * n
    for step in range(ITERS):
        image = apply_normal(direction)
        alpha = gamma / dot(direction, image, 1)
        solved = [a + alpha * b for a, b in zip(solved, direction)]
        if step + 1 < ITERS:
            gradient = [a - alpha * b for a, b in zip(gradient, image)]
            steer = forward(gradient)
            gamma_new = dot(steer, steer, 0)
            ratio = gamma_new / gamma
            direction = [a + ratio * b for a, b in zip(backward(steer), direction)]
            gamma = gamma_new
    left = []
    for level in range(n):
        coef_ref[:, blk(level)] = solved[level]
        left.append(effects[level] - solved[level])
    parts = split3(jnp.concatenate(left, axis=0))
    weights = jnp.concatenate(list(parts) + [jnp.zeros((4, COV), F32)], axis=0).astype(BF16)
    values = lax.dot_general(
        weights, cov_ref[...], (((1,), (1,)), ((), ())), preferred_element_type=F32
    )
    codes = codes_ref[...]
    resid = noise_ref[...]
    for level in range(n):
        value = values[level : level + 1] + values[4 + level : 5 + level] + values[8 + level : 9 + level]
        resid = resid + jnp.where(codes == level, value, 0.0)
    resid_ref[...] = resid
    for copy in stores:
        copy.wait()


def solve(sketch, square, extra, effects, covariates, codes, noise):
    vmem = pl.BlockSpec(memory_space=pltpu.VMEM)
    hbm = pl.BlockSpec(memory_space=pltpu.HBM)
    return pl.pallas_call(
        solve_kernel,
        out_shape=(
            jax.ShapeDtypeStruct((1, COLS), F32),
            jax.ShapeDtypeStruct((1, ROWS), F32),
            jax.ShapeDtypeStruct((COLS, COLS), F32),
        ),
        in_specs=[vmem] * 3 + [hbm] * 4,
        out_specs=(vmem, vmem, hbm),
        scratch_shapes=[
            pltpu.VMEM((LEVELS, COV, COLS), F32),
            pltpu.VMEM((LEVELS, COV, COLS), F32),
            pltpu.VMEM((COLS, COLS), F32),
            pltpu.VMEM((1, COLS), F32),
            pltpu.VMEM((ROWS, COV), BF16),
            pltpu.VMEM((1, ROWS), jnp.int32),
            pltpu.VMEM((1, ROWS), F32),
            pltpu.SemaphoreType.DMA((4,)),
            pltpu.SemaphoreType.DMA((LEVELS,)),
        ],
        compiler_params=pltpu.CompilerParams(vmem_limit_bytes=40 << 20),
        name="solve",
    )(sketch, square, extra, effects, covariates, codes, noise)


def body(covariates, level_codes, sign_bits, sample_rows, effects, noise):
    def fixed(value):
        return pltpu.with_memory_space_constraint(value, pltpu.HBM)

    covariates = fixed(covariates)
    codes = fixed(level_codes.reshape(1, ROWS))
    noise = fixed(noise.reshape(1, ROWS))
    sketch, square, extra = gather(
        fixed(sample_rows), covariates, codes, fixed(sign_bits.reshape(1, ROWS)), noise
    )
    coef, resid, factor = solve(
        sketch.reshape(SKETCH, COLS), square.reshape(2, COV, COV), extra,
        fixed(effects.reshape(1, COLS)), covariates, codes, noise,
    )
    return coef.reshape(COLS), resid.reshape(ROWS), factor


def solution(mesh):
    rows = P(("wide", "narrow"))
    return jax.shard_map(
        body,
        mesh=mesh,
        in_specs=(P(("wide", "narrow"), None), rows, rows, rows, P(), rows),
        out_specs=(P(), rows, P()),
        check_vma=False,
    )
```

```python
import functools
import math

import jax
import jax.numpy as jnp
from jax import lax
from jax.experimental import pallas as pl
from jax.experimental.pallas import tpu as pltpu
from jax.sharding import PartitionSpec as P

COV = 128
LEVELS = 4
COLS = COV * LEVELS
ROWS = 2048
HB = 256
SKETCH = 1024
SAMP = 4
ITERS = 4
GROUP = 8
NZ = 8
NX = 4
NY = 4
EXTRA = 8
LANES = 128

HALF_ROOT = math.sqrt(0.5)
HIGH = lax.Precision.HIGHEST
MESH = pl.DeviceIdType.MESH
F32 = jnp.float32
BF16 = jnp.bfloat16


def iota(shape, axis):
    return lax.broadcasted_iota(jnp.int32, shape, axis)


def split3(value):
    high = value.astype(BF16)
    rest = value - high.astype(F32)
    middle = rest.astype(BF16)
    low = (rest - middle.astype(F32)).astype(BF16)
    return high.astype(F32), middle.astype(F32), low.astype(F32)


def ring(offset, size):
    return min(offset, size - offset)


Z_FAR = sorted(range(1, NZ), key=lambda o: -ring(o, NZ))
FOUR_FAR = (2, 1, 3)
MIX_FAR = sorted(
    [(dx, dc) for dx in range(4) for dc in range(2) if (dx, dc) != (0, 0)],
    key=lambda o: -(ring(o[0], 4) + o[1]),
)


def gather_kernel(
    samp_hbm, cov_hbm, codes_hbm, bits_hbm, noise_hbm,
    sketch_ref, square_ref, extra_ref,
    samp_ref, cov_ref, codes_ref, bits_ref, noise_ref,
    own, asked, picks, lhs, sent, held, rowz,
    halves, half_in, pieces, piece_in, row_in, col_in,
    send, recv, load,
):
    loads = [
        pltpu.make_async_copy(src, dst, load.at[i])
        for i, (src, dst) in enumerate(
            [
                (samp_hbm, samp_ref), (cov_hbm, cov_ref), (codes_hbm, codes_ref),
                (bits_hbm, bits_ref), (noise_hbm, noise_ref),
            ]
        )
    ]
    for copy in loads:
        copy.start()
    wide = lax.axis_index("wide")
    z = lax.axis_index("narrow")
    core = lax.rem(wide, 2)
    q = wide // 2
    x = lax.rem(q, 4)
    y = q // 4
    member = lax.rem(wide, GROUP)
    base = wide - member
    sibling = wide + 1 - 2 * core
    mix_peers = [lax.rem(x + dx, 4) * 2 + lax.rem(core + dc, 2) for dx, dc in MIX_FAR]
    z_peers = [lax.rem(z + o, NZ) for o in Z_FAR]
    x_peers = [(y * 4 + lax.rem(x + o, 4)) * 2 + core for o in FOUR_FAR]
    y_peers = [(lax.rem(y + o, 4) * 4 + x) * 2 + core for o in FOUR_FAR]

    slots = iter(range(N_COPIES))

    def remote(src, dst, to_wide, to_z):
        slot = next(slots)
        return pltpu.make_async_remote_copy(
            src_ref=src, dst_ref=dst, send_sem=send.at[slot], recv_sem=recv.at[slot],
            device_id=(to_wide, to_z), device_id_type=MESH,
        )

    barrier = pltpu.get_barrier_semaphore()
    for peer in z_peers:
        pl.semaphore_signal(barrier, inc=1, device_id=(wide, peer), device_id_type=MESH)
    for peer in y_peers:
        pl.semaphore_signal(barrier, inc=1, device_id=(peer, z), device_id_type=MESH)
    for peer in mix_peers:
        pl.semaphore_signal(barrier, inc=1, device_id=(base + peer, z), device_id_type=MESH)

    loads[0].wait()
    for k in range(8):
        own[k : k + 1, :] = jnp.full((1, LANES), samp_ref[k % SAMP], jnp.int32)
    asked[member] = own[...]
    pl.semaphore_wait(barrier, len(Z_FAR) + len(FOUR_FAR) + len(MIX_FAR))

    ask = [remote(own, asked.at[member], base + peer, z) for peer in mix_peers]
    for copy in ask:
        copy.start()

    for copy in loads[1:]:
        copy.wait()
    codes = codes_ref[...]
    flip = cov_ref[...].astype(F32).T
    masks = [(codes == level).astype(F32) for level in range(LEVELS)]
    for level in range(LEVELS):
        lhs[level * COV : (level + 1) * COV, :] = (flip * masks[level]).astype(BF16)
    parts = split3(noise_ref[...])
    shadow_rows = [part * mask for part in parts for mask in masks]
    shadow_rows = jnp.concatenate(shadow_rows + [jnp.zeros((4, ROWS), F32)], axis=0)
    normal = jnp.dot(lhs[...], cov_ref[...], preferred_element_type=F32)
    shadow = jnp.dot(shadow_rows.astype(BF16), cov_ref[...], preferred_element_type=F32)
    shadow = shadow[0:4] + shadow[4:8] + shadow[8:12]
    sub = iota((COV, COV), 0)
    lane = iota((COV, COV), 1)
    diagonals = []
    for pair in range(2):
        even = normal[2 * pair * COV : (2 * pair + 1) * COV]
        odd = normal[(2 * pair + 1) * COV : (2 * pair + 2) * COV]
        halves[pair, 0:COV, :] = jnp.where(lane >= sub, even, odd)
        diagonals.append(jnp.sum(jnp.where(lane == sub, odd, 0.0), axis=0, keepdims=True))
    extra = jnp.concatenate([shadow] + diagonals + [jnp.zeros((2, COV), F32)], axis=0)
    halves[0, COV:, :] = extra
    halves[1, COV:, :] = extra
    a_core = remote(halves.at[1 - core], half_in, sibling, z)
    a_core.start()

    for copy in ask:
        copy.wait_recv()
    want = jnp.concatenate([asked[i] for i in range(GROUP)], axis=0)
    shape = (GROUP * 8, LANES)
    common = want & iota(shape, 1)
    common = common ^ (common >> 4)
    common = common ^ (common >> 2)
    low = common ^ (common >> 1)
    top = (want >> 7) & 1
    block = want >> 8
    upper_half = (iota(shape, 0) // SAMP) & 1
    for chunk in range(ROWS // LANES):
        span = slice(chunk * LANES, (chunk + 1) * LANES)
        parity = low ^ bits_ref[:, span]
        if chunk % 2:
            parity = parity ^ top
        sign = (1 - 2 * (parity & 1)).astype(F32)
        sign = jnp.where(block == chunk // 2, sign, 0.0)
        here = codes_ref[:, span]
        for pair in range(2):
            value = jnp.where(here == 2 * pair + upper_half, sign, 0.0)
            picks[pair * 64 : (pair + 1) * 64, span] = value.astype(BF16)
    local = jnp.dot(picks[...], cov_ref[...], preferred_element_type=F32)
    local = local * (1.0 / math.sqrt(HB))
    for i in range(GROUP):
        spots = [pair * 64 + i * 8 + SAMP * half for pair in range(2) for half in range(2)]
        sent[i] = jnp.concatenate([local[at : at + SAMP] for at in spots], axis=1).astype(BF16)
    held[member] = sent[member]
    rows = [remote(sent.at[peer], held.at[member], base + peer, z) for peer in mix_peers]
    for copy in rows:
        copy.start()

    a_core.wait_recv()
    mine = halves[core] + half_in[...]
    for i in range(NZ):
        pieces[i] = jnp.concatenate([mine[i * 16 : (i + 1) * 16], mine[COV:]], axis=0)
    piece_in[z] = pieces[z]
    a_z = [remote(pieces.at[peer], piece_in.at[z], wide, peer) for peer in z_peers]
    for copy in a_z:
        copy.start()

    for copy in rows:
        copy.wait_recv()
    level_rows = [held[i].astype(F32) for i in range(GROUP)]
    for place in range(3):
        side = (1 - 2 * lax.rem(wide // (2**place), 2)).astype(F32)
        level_rows = [
            ((level_rows[i] + side * level_rows[i + 1]) * HALF_ROOT).astype(BF16).astype(F32)
            for i in range(0, len(level_rows), 2)
        ]
    rowz[z] = level_rows[0].astype(BF16)
    s_z = [remote(rowz.at[z], rowz.at[z], wide, peer) for peer in z_peers]
    for copy in s_z:
        copy.start()

    for copy in a_z:
        copy.wait_recv()
    total = piece_in[0]
    for i in range(1, NZ):
        total = total + piece_in[i]
    row_in[x] = total
    a_x = [remote(row_in.at[x], row_in.at[x], peer, z) for peer in x_peers]
    for copy in a_x:
        copy.start()

    for copy in s_z:
        copy.wait_recv()
    stack = jnp.concatenate([rowz[i].astype(F32) for i in range(NZ)], axis=0).astype(BF16)
    sketch_ref[0, core, y, x] = stack[:16]
    sketch_ref[1, core, x, y] = stack[16:]
    first = sketch_ref.at[0, core, y, x]
    second = sketch_ref.at[1, core, x, y]
    s_first = [remote(first, first, peer, z) for peer in x_peers]
    s_second = [remote(second, second, peer, z) for peer in y_peers]
    for one, two in zip(s_first, s_second):
        one.start()
        two.start()

    for copy in a_x:
        copy.wait_recv()
    total = row_in[0]
    for i in range(1, NX):
        total = total + row_in[i]
    col_in[y] = total
    a_y = [remote(col_in.at[y], col_in.at[y], peer, z) for peer in y_peers]
    for copy in a_y:
        copy.start()

    for copy in s_first + s_second:
        copy.wait_recv()
    line = sketch_ref.at[0, core, y]
    other = sketch_ref.at[1, core, x]
    s_line = [remote(line, line, peer, z) for peer in y_peers]
    s_other = [remote(other, other, peer, z) for peer in x_peers]
    for one, two in zip(s_line, s_other):
        one.start()
        two.start()
    s_core = [remote(line, line, sibling, z), remote(other, other, sibling, z)]
    for copy in s_core:
        copy.start()

    for copy in a_y:
        copy.wait_recv()
    total = col_in[0]
    for i in range(1, NY):
        total = total + col_in[i]
    extra_ref[...] = total[16:]
    square_ref[core, z] = total[:16]
    mine = square_ref.at[core, z]
    a_out = [remote(mine, mine, wide, peer) for peer in z_peers]
    for copy in a_out:
        copy.start()

    def onward(index):
        s_line[index].wait_recv()
        passed = sketch_ref.at[0, core, lax.rem(y - FOUR_FAR[index] + 4, 4)]
        copy = remote(passed, passed, sibling, z)
        copy.start()
        s_core.append(copy)
        s_other[index].wait_recv()
        passed = sketch_ref.at[1, core, lax.rem(x - FOUR_FAR[index] + 4, 4)]
        copy = remote(passed, passed, sibling, z)
        copy.start()
        s_core.append(copy)

    onward(1)
    onward(2)
    for copy in a_out:
        copy.wait_recv()
    a_last = remote(square_ref.at[core], square_ref.at[core], sibling, z)
    a_last.start()
    onward(0)
    a_last.wait_recv()
    for copy in s_core:
        copy.wait_recv()
    sums = [a_core] + a_z + a_x + a_y + a_out + [a_last]
    for copy in ask + rows + s_z + s_first + s_second + s_line + s_other + s_core + sums:
        copy.wait_send()


N_COPIES = 7 + 1 + 7 + 7 + 7 + 3 + 6 + 3 + 6 + 8 + 7 + 1


def gather(samples, covariates, codes, bits, noise):
    vmem = pl.BlockSpec(memory_space=pltpu.VMEM)
    hbm = pl.BlockSpec(memory_space=pltpu.HBM)
    return pl.pallas_call(
        gather_kernel,
        out_shape=(
            jax.ShapeDtypeStruct((2, 2, 4, 4, 16, COLS), BF16),
            jax.ShapeDtypeStruct((2, NZ, 16, COV), F32),
            jax.ShapeDtypeStruct((EXTRA, COV), F32),
        ),
        in_specs=[hbm] * 5,
        out_specs=(vmem, vmem, vmem),
        scratch_shapes=[
            pltpu.SMEM((SAMP,), jnp.int32),
            pltpu.VMEM((ROWS, COV), BF16),
            pltpu.VMEM((1, ROWS), jnp.int32),
            pltpu.VMEM((1, ROWS), jnp.int32),
            pltpu.VMEM((1, ROWS), F32),
            pltpu.VMEM((8, LANES), jnp.int32),
            pltpu.VMEM((GROUP, 8, LANES), jnp.int32),
            pltpu.VMEM((2 * 64, ROWS), BF16),
            pltpu.VMEM((COLS, ROWS), BF16),
            pltpu.VMEM((GROUP, SAMP, COLS), BF16),
            pltpu.VMEM((GROUP, SAMP, COLS), BF16),
            pltpu.VMEM((NZ, SAMP, COLS), BF16),
            pltpu.VMEM((2, COV + EXTRA, COV), F32),
            pltpu.VMEM((COV + EXTRA, COV), F32),
            pltpu.VMEM((NZ, 16 + EXTRA, COV), F32),
            pltpu.VMEM((NZ, 16 + EXTRA, COV), F32),
            pltpu.VMEM((NX, 16 + EXTRA, COV), F32),
            pltpu.VMEM((NY, 16 + EXTRA, COV), F32),
            pltpu.SemaphoreType.DMA((N_COPIES,)),
            pltpu.SemaphoreType.DMA((N_COPIES,)),
            pltpu.SemaphoreType.DMA((5,)),
        ],
        compiler_params=pltpu.CompilerParams(
            collective_id=0, has_side_effects=True, vmem_limit_bytes=40 << 20
        ),
        name="gather_sketch",
    )(samples, covariates, codes, bits, noise)


def spread(value, index):
    return jnp.broadcast_to(value[index : index + 1, :], value.shape)


def column(value, index):
    return jnp.broadcast_to(value[:, index : index + 1], value.shape)


def invert_factor(matrix, ahead=2):
    count = COV // 8
    rows = [matrix[8 * t : 8 * t + 8, :] for t in range(count)]
    sub = iota((8, COV), 0)
    lane = iota((8, COV), 1)
    for p in range(count):
        first = 8 * p
        panel = (lane >= first) & (lane < first + 8)
        near = range(p, min(p + 1 + ahead, count))
        own = {t: [column(rows[t], first + i) for i in range(8)] for t in near}
        left = [[spread(own[p][c], a) for c in range(a + 1)] for a in range(8)]
        rows[p] = jnp.where(panel, jnp.where(lane == first + sub, 1.0, 0.0), rows[p])
        start = [spread(rows[p], i) for i in range(8)]
        root = []
        low = [[None] * 8 for _ in range(8)]
        for i in range(8):
            root.append(lax.rsqrt(left[i][i]))
            for a in range(i + 1, 8):
                low[a][i] = left[a][i] * root[i]
            for a in range(i + 1, 8):
                for c in range(i + 1, a + 1):
                    left[a][c] = left[a][c] - low[a][i] * low[c][i]
        row = []
        for i in range(8):
            value = start[i]
            for k in range(i):
                value = value - low[i][k] * row[k]
            row.append(value * root[i])
        value = row[7]
        for i in range(7):
            value = jnp.where(sub == i, row[i], value)
        rows[p] = value
        far = range(p + 1 + ahead, count)
        if len(far):
            high, middle, small = split3(value)
            one = jnp.concatenate([high, high, high, middle, middle, small], axis=0).astype(BF16)
            two = jnp.concatenate([high, middle, small, high, middle, high], axis=0).astype(BF16)
            change = lax.dot_general(
                one, two, (((0,), (0,)), ((), ())), preferred_element_type=F32
            )
        for t in near[1:]:
            value = jnp.where(panel, 0.0, rows[t])
            scales = []
            for i in range(8):
                scale = own[t][i]
                for k in range(i):
                    scale = scale - scales[k] * low[i][k]
                scales.append(scale * root[i])
                value = value - scales[i] * row[i]
            rows[t] = value
        for t in far:
            rows[t] = jnp.where(panel, 0.0, rows[t]) - change[8 * t : 8 * t + 8, :]
    for p in range(count):
        rows[p] = jnp.where(lane <= 8 * p + sub, rows[p], 0.0)
    return jnp.concatenate(rows, axis=0)


def blk(index):
    return slice(index * COV, (index + 1) * COV)


def solve_kernel(
    sketch_ref, square_ref, extra_ref, effects_hbm, cov_hbm, codes_hbm, noise_hbm,
    coef_ref, resid_ref, factor_hbm, gram, inverse,
    factor_ref, effects_ref, cov_ref, codes_ref, noise_ref, load, store,
):
    loads = [
        pltpu.make_async_copy(src, dst, load.at[i])
        for i, (src, dst) in enumerate(
            [
                (effects_hbm, effects_ref), (cov_hbm, cov_ref), (codes_hbm, codes_ref),
                (noise_hbm, noise_ref),
            ]
        )
    ]
    for copy in loads:
        copy.start()
    stores = []
    n = LEVELS
    sub = iota((COV, COV), 0)
    lane = iota((COV, COV), 1)
    scale = math.sqrt(LEVELS / SKETCH)
    for k in range(n):
        gram[k, :, k * COV :] = lax.dot_general(
            sketch_ref[:, blk(k)], sketch_ref[:, k * COV :], (((0,), (0,)), ((), ())),
            preferred_element_type=F32,
        )
    for k in range(n):
        corner = invert_factor(gram[k, :, blk(k)])
        inverse[k, :, blk(k)] = corner
        product = jnp.dot(corner, gram[k], precision=HIGH, preferred_element_type=F32)
        if k:
            inverse[k, :, : k * COV] = product[:, : k * COV]
            factor_ref[blk(k), : k * COV] = jnp.zeros((COV, k * COV), F32)
        factor_ref[blk(k), blk(k)] = jnp.where(lane >= sub, product[:, blk(k)], 0.0) * scale
        if k + 1 < n:
            factor_ref[blk(k), (k + 1) * COV :] = product[:, (k + 1) * COV :] * scale
        part = pltpu.make_async_copy(factor_ref.at[blk(k)], factor_hbm.at[blk(k)], store.at[k])
        part.start()
        stores.append(part)
        for i in range(k + 1, n):
            back = product[:, blk(i)].T
            change = jnp.dot(back, product[:, i * COV :], precision=HIGH, preferred_element_type=F32)
            gram[i, :, i * COV :] = gram[i, :, i * COV :] - change
        for i in range(k + 1, n):
            back = product[:, blk(i)].T
            gram[i, :, blk(k)] = -jnp.dot(back, corner, precision=HIGH, preferred_element_type=F32)
            if k:
                change = jnp.dot(back, product[:, : k * COV], precision=HIGH, preferred_element_type=F32)
                gram[i, :, : k * COV] = gram[i, :, : k * COV] - change

    normal = []
    for pair in range(2):
        square = square_ref[pair]
        turned = square.T
        diagonal = extra_ref[4 + pair : 5 + pair, :]
        normal.append(jnp.where(lane >= sub, square, turned))
        normal.append(jnp.where(lane < sub, square, jnp.where(lane > sub, turned, diagonal)))

    def apply_normal(rows):
        out = []
        for level in range(n):
            column = jnp.sum(normal[level] * rows[level], axis=1, keepdims=True)
            out.append(jnp.sum(jnp.where(lane == sub, column, 0.0), axis=0, keepdims=True))
        return out

    def forward(rows):
        out = []
        for k in range(n):
            acc = inverse[k, :, blk(0)] * rows[0]
            for c in range(1, k + 1):
                acc = acc + inverse[k, :, blk(c)] * rows[c]
            out.append(jnp.sum(acc, axis=1, keepdims=True))
        return out

    def backward(columns):
        out = []
        for c in range(n):
            acc = inverse[c, :, blk(c)] * columns[c]
            for k in range(c + 1, n):
                acc = acc + inverse[k, :, blk(c)] * columns[k]
            out.append(jnp.sum(acc, axis=0, keepdims=True))
        return out

    def dot(left, right, axis):
        acc = left[0] * right[0]
        for a, b in zip(left[1:], right[1:]):
            acc = acc + a * b
        return jnp.sum(acc, axis=axis, keepdims=True)

    for copy in loads:
        copy.wait()
    effects = [effects_ref[:, blk(level)] for level in range(n)]
    gradient = [
        image + extra_ref[level : level + 1, :] for level, image in enumerate(apply_normal(effects))
    ]
    steer = forward(gradient)
    gamma = dot(steer, steer, 0)
    direction = backward(steer)
    solved = [jnp.zeros((1, COV), F32)] * n
    for step in range(ITERS):
        image = apply_normal(direction)
        alpha = gamma / dot(direction, image, 1)
        solved = [a + alpha * b for a, b in zip(solved, direction)]
        if step + 1 < ITERS:
            gradient = [a - alpha * b for a, b in zip(gradient, image)]
            steer = forward(gradient)
            gamma_new = dot(steer, steer, 0)
            ratio = gamma_new / gamma
            direction = [a + ratio * b for a, b in zip(backward(steer), direction)]
            gamma = gamma_new
    left = []
    for level in range(n):
        coef_ref[:, blk(level)] = solved[level]
        left.append(effects[level] - solved[level])
    parts = split3(jnp.concatenate(left, axis=0))
    weights = jnp.concatenate(list(parts) + [jnp.zeros((4, COV), F32)], axis=0).astype(BF16)
    values = lax.dot_general(
        weights, cov_ref[...], (((1,), (1,)), ((), ())), preferred_element_type=F32
    )
    codes = codes_ref[...]
    resid = noise_ref[...]
    for level in range(n):
        value = values[level : level + 1] + values[4 + level : 5 + level] + values[8 + level : 9 + level]
        resid = resid + jnp.where(codes == level, value, 0.0)
    resid_ref[...] = resid
    for copy in stores:
        copy.wait()


def solve(sketch, square, extra, effects, covariates, codes, noise):
    vmem = pl.BlockSpec(memory_space=pltpu.VMEM)
    hbm = pl.BlockSpec(memory_space=pltpu.HBM)
    return pl.pallas_call(
        solve_kernel,
        out_shape=(
            jax.ShapeDtypeStruct((1, COLS), F32),
            jax.ShapeDtypeStruct((1, ROWS), F32),
            jax.ShapeDtypeStruct((COLS, COLS), F32),
        ),
        in_specs=[vmem] * 3 + [hbm] * 4,
        out_specs=(vmem, vmem, hbm),
        scratch_shapes=[
            pltpu.VMEM((LEVELS, COV, COLS), F32),
            pltpu.VMEM((LEVELS, COV, COLS), F32),
            pltpu.VMEM((COLS, COLS), F32),
            pltpu.VMEM((1, COLS), F32),
            pltpu.VMEM((ROWS, COV), BF16),
            pltpu.VMEM((1, ROWS), jnp.int32),
            pltpu.VMEM((1, ROWS), F32),
            pltpu.SemaphoreType.DMA((4,)),
            pltpu.SemaphoreType.DMA((LEVELS,)),
        ],
        compiler_params=pltpu.CompilerParams(vmem_limit_bytes=40 << 20),
        name="solve",
    )(sketch, square, extra, effects, covariates, codes, noise)


def body(covariates, level_codes, sign_bits, sample_rows, effects, noise):
    def fixed(value):
        return pltpu.with_memory_space_constraint(value, pltpu.HBM)

    covariates = fixed(covariates)
    codes = fixed(level_codes.reshape(1, ROWS))
    noise = fixed(noise.reshape(1, ROWS))
    sketch, square, extra = gather(
        fixed(sample_rows), covariates, codes, fixed(sign_bits.reshape(1, ROWS)), noise
    )
    coef, resid, factor = solve(
        sketch.reshape(SKETCH, COLS), square.reshape(2, COV, COV), extra,
        fixed(effects.reshape(1, COLS)), covariates, codes, noise,
    )
    return coef.reshape(COLS), resid.reshape(ROWS), factor


def solution(mesh):
    rows = P(("wide", "narrow"))
    return jax.shard_map(
        body,
        mesh=mesh,
        in_specs=(P(("wide", "narrow"), None), rows, rows, rows, P(), rows),
        out_specs=(P(), rows, P()),
        check_vma=False,
    )
```

```python
import functools
import math

import jax
import jax.numpy as jnp
from jax import lax
from jax.experimental import pallas as pl
from jax.experimental.pallas import tpu as pltpu
from jax.sharding import PartitionSpec as P

COV = 128
LEVELS = 4
COLS = COV * LEVELS
ROWS = 2048
HB = 256
SKETCH = 1024
SAMP = 4
ITERS = 4
GROUP = 8
NZ = 8
NX = 4
NY = 4
EXTRA = 8
LANES = 128

HALF_ROOT = math.sqrt(0.5)
HIGH = lax.Precision.HIGHEST
MESH = pl.DeviceIdType.MESH
F32 = jnp.float32
BF16 = jnp.bfloat16


def iota(shape, axis):
    return lax.broadcasted_iota(jnp.int32, shape, axis)


def split3(value):
    high = value.astype(BF16)
    rest = value - high.astype(F32)
    middle = rest.astype(BF16)
    low = (rest - middle.astype(F32)).astype(BF16)
    return high.astype(F32), middle.astype(F32), low.astype(F32)


def ring(offset, size):
    return min(offset, size - offset)


Z_FAR = sorted(range(1, NZ), key=lambda o: -ring(o, NZ))
FOUR_FAR = (2, 1, 3)
MIX_FAR = sorted(
    [(dx, dc) for dx in range(4) for dc in range(2) if (dx, dc) != (0, 0)],
    key=lambda o: -(ring(o[0], 4) + o[1]),
)


def gather_kernel(
    samp_hbm, cov_hbm, codes_hbm, bits_hbm, noise_hbm,
    sketch_ref, square_ref, extra_ref,
    samp_ref, cov_ref, codes_ref, bits_ref, noise_ref,
    own, asked, picks, lhs, sent, held, rowz,
    halves, half_in, pieces, piece_in, row_in, col_in,
    send, recv, load,
):
    loads = [
        pltpu.make_async_copy(src, dst, load.at[i])
        for i, (src, dst) in enumerate(
            [
                (samp_hbm, samp_ref), (cov_hbm, cov_ref), (codes_hbm, codes_ref),
                (bits_hbm, bits_ref), (noise_hbm, noise_ref),
            ]
        )
    ]
    for copy in loads:
        copy.start()
    wide = lax.axis_index("wide")
    z = lax.axis_index("narrow")
    core = lax.rem(wide, 2)
    q = wide // 2
    x = lax.rem(q, 4)
    y = q // 4
    member = lax.rem(wide, GROUP)
    base = wide - member
    sibling = wide + 1 - 2 * core
    mix_peers = [lax.rem(x + dx, 4) * 2 + lax.rem(core + dc, 2) for dx, dc in MIX_FAR]
    z_peers = [lax.rem(z + o, NZ) for o in Z_FAR]
    x_peers = [(y * 4 + lax.rem(x + o, 4)) * 2 + core for o in FOUR_FAR]
    y_peers = [(lax.rem(y + o, 4) * 4 + x) * 2 + core for o in FOUR_FAR]

    slots = iter(range(N_COPIES))

    def remote(src, dst, to_wide, to_z):
        slot = next(slots)
        return pltpu.make_async_remote_copy(
            src_ref=src, dst_ref=dst, send_sem=send.at[slot], recv_sem=recv.at[slot],
            device_id=(to_wide, to_z), device_id_type=MESH,
        )

    barrier = pltpu.get_barrier_semaphore()
    for peer in z_peers:
        pl.semaphore_signal(barrier, inc=1, device_id=(wide, peer), device_id_type=MESH)
    for peer in y_peers:
        pl.semaphore_signal(barrier, inc=1, device_id=(peer, z), device_id_type=MESH)
    for peer in mix_peers:
        pl.semaphore_signal(barrier, inc=1, device_id=(base + peer, z), device_id_type=MESH)

    loads[0].wait()
    for k in range(8):
        own[k : k + 1, :] = jnp.full((1, LANES), samp_ref[k % SAMP], jnp.int32)
    asked[member] = own[...]
    pl.semaphore_wait(barrier, len(Z_FAR) + len(FOUR_FAR) + len(MIX_FAR))

    ask = [remote(own, asked.at[member], base + peer, z) for peer in mix_peers]
    for copy in ask:
        copy.start()

    for copy in loads[1:]:
        copy.wait()
    codes = codes_ref[...]
    flip = cov_ref[...].astype(F32).T
    masks = [(codes == level).astype(F32) for level in range(LEVELS)]
    for level in range(LEVELS):
        lhs[level * COV : (level + 1) * COV, :] = (flip * masks[level]).astype(BF16)
    parts = split3(noise_ref[...])
    shadow_rows = [part * mask for part in parts for mask in masks]
    shadow_rows = jnp.concatenate(shadow_rows + [jnp.zeros((4, ROWS), F32)], axis=0)
    normal = jnp.dot(lhs[...], cov_ref[...], preferred_element_type=F32)
    shadow = jnp.dot(shadow_rows.astype(BF16), cov_ref[...], preferred_element_type=F32)
    shadow = shadow[0:4] + shadow[4:8] + shadow[8:12]
    sub = iota((COV, COV), 0)
    lane = iota((COV, COV), 1)
    diagonals = []
    for pair in range(2):
        even = normal[2 * pair * COV : (2 * pair + 1) * COV]
        odd = normal[(2 * pair + 1) * COV : (2 * pair + 2) * COV]
        halves[pair, 0:COV, :] = jnp.where(lane >= sub, even, odd)
        diagonals.append(jnp.sum(jnp.where(lane == sub, odd, 0.0), axis=0, keepdims=True))
    extra = jnp.concatenate([shadow] + diagonals + [jnp.zeros((2, COV), F32)], axis=0)
    halves[0, COV:, :] = extra
    halves[1, COV:, :] = extra
    a_core = remote(halves.at[1 - core], half_in, sibling, z)
    a_core.start()

    for copy in ask:
        copy.wait_recv()
    want = jnp.concatenate([asked[i] for i in range(GROUP)], axis=0)
    shape = (GROUP * 8, LANES)
    common = want & iota(shape, 1)
    common = common ^ (common >> 4)
    common = common ^ (common >> 2)
    low = common ^ (common >> 1)
    top = (want >> 7) & 1
    block = want >> 8
    upper_half = (iota(shape, 0) // SAMP) & 1
    for chunk in range(ROWS // LANES):
        span = slice(chunk * LANES, (chunk + 1) * LANES)
        parity = low ^ bits_ref[:, span]
        if chunk % 2:
            parity = parity ^ top
        sign = (1 - 2 * (parity & 1)).astype(F32)
        sign = jnp.where(block == chunk // 2, sign, 0.0)
        here = codes_ref[:, span]
        for pair in range(2):
            value = jnp.where(here == 2 * pair + upper_half, sign, 0.0)
            picks[pair * 64 : (pair + 1) * 64, span] = value.astype(BF16)
    local = jnp.dot(picks[...], cov_ref[...], preferred_element_type=F32)
    local = local * (1.0 / math.sqrt(HB))
    for i in range(GROUP):
        spots = [pair * 64 + i * 8 + SAMP * half for pair in range(2) for half in range(2)]
        sent[i] = jnp.concatenate([local[at : at + SAMP] for at in spots], axis=1).astype(BF16)
    held[member] = sent[member]
    rows = [remote(sent.at[peer], held.at[member], base + peer, z) for peer in mix_peers]
    for copy in rows:
        copy.start()

    a_core.wait_recv()
    mine = halves[core] + half_in[...]
    for i in range(NZ):
        pieces[i] = jnp.concatenate([mine[i * 16 : (i + 1) * 16], mine[COV:]], axis=0)
    piece_in[z] = pieces[z]
    a_z = [remote(pieces.at[peer], piece_in.at[z], wide, peer) for peer in z_peers]
    for copy in a_z:
        copy.start()

    for copy in rows:
        copy.wait_recv()
    level_rows = [held[i].astype(F32) for i in range(GROUP)]
    for place in range(3):
        side = (1 - 2 * lax.rem(wide // (2**place), 2)).astype(F32)
        level_rows = [
            ((level_rows[i] + side * level_rows[i + 1]) * HALF_ROOT).astype(BF16).astype(F32)
            for i in range(0, len(level_rows), 2)
        ]
    rowz[z] = level_rows[0].astype(BF16)
    s_z = [remote(rowz.at[z], rowz.at[z], wide, peer) for peer in z_peers]
    for copy in s_z:
        copy.start()

    for copy in a_z:
        copy.wait_recv()
    total = piece_in[0]
    for i in range(1, NZ):
        total = total + piece_in[i]
    row_in[x] = total
    a_x = [remote(row_in.at[x], row_in.at[x], peer, z) for peer in x_peers]
    for copy in a_x:
        copy.start()

    for copy in s_z:
        copy.wait_recv()
    stack = jnp.concatenate([rowz[i].astype(F32) for i in range(NZ)], axis=0).astype(BF16)
    sketch_ref[0, core, y, x] = stack[:16]
    sketch_ref[1, core, x, y] = stack[16:]
    first = sketch_ref.at[0, core, y, x]
    second = sketch_ref.at[1, core, x, y]
    s_first = [remote(first, first, peer, z) for peer in x_peers]
    s_second = [remote(second, second, peer, z) for peer in y_peers]
    for one, two in zip(s_first, s_second):
        one.start()
        two.start()

    for copy in a_x:
        copy.wait_recv()
    total = row_in[0]
    for i in range(1, NX):
        total = total + row_in[i]
    col_in[y] = total
    a_y = [remote(col_in.at[y], col_in.at[y], peer, z) for peer in y_peers]
    for copy in a_y:
        copy.start()

    for copy in s_first + s_second:
        copy.wait_recv()
    line = sketch_ref.at[0, core, y]
    other = sketch_ref.at[1, core, x]
    s_line = [remote(line, line, peer, z) for peer in y_peers]
    s_other = [remote(other, other, peer, z) for peer in x_peers]
    for one, two in zip(s_line, s_other):
        one.start()
        two.start()
    s_core = [remote(line, line, sibling, z), remote(other, other, sibling, z)]
    for copy in s_core:
        copy.start()

    for copy in a_y:
        copy.wait_recv()
    total = col_in[0]
    for i in range(1, NY):
        total = total + col_in[i]
    extra_ref[...] = total[16:]
    square_ref[core, z] = total[:16]
    mine = square_ref.at[core, z]
    a_out = [remote(mine, mine, wide, peer) for peer in z_peers]
    for copy in a_out:
        copy.start()

    def onward(index):
        s_line[index].wait_recv()
        passed = sketch_ref.at[0, core, lax.rem(y - FOUR_FAR[index] + 4, 4)]
        copy = remote(passed, passed, sibling, z)
        copy.start()
        s_core.append(copy)
        s_other[index].wait_recv()
        passed = sketch_ref.at[1, core, lax.rem(x - FOUR_FAR[index] + 4, 4)]
        copy = remote(passed, passed, sibling, z)
        copy.start()
        s_core.append(copy)

    onward(1)
    onward(2)
    for copy in a_out:
        copy.wait_recv()
    a_last = remote(square_ref.at[core], square_ref.at[core], sibling, z)
    a_last.start()
    onward(0)
    a_last.wait_recv()
    for copy in s_core:
        copy.wait_recv()
    sums = [a_core] + a_z + a_x + a_y + a_out + [a_last]
    for copy in ask + rows + s_z + s_first + s_second + s_line + s_other + s_core + sums:
        copy.wait_send()


N_COPIES = 7 + 1 + 7 + 7 + 7 + 3 + 6 + 3 + 6 + 8 + 7 + 1


def gather(samples, covariates, codes, bits, noise):
    vmem = pl.BlockSpec(memory_space=pltpu.VMEM)
    hbm = pl.BlockSpec(memory_space=pltpu.HBM)
    return pl.pallas_call(
        gather_kernel,
        out_shape=(
            jax.ShapeDtypeStruct((2, 2, 4, 4, 16, COLS), BF16),
            jax.ShapeDtypeStruct((2, NZ, 16, COV), F32),
            jax.ShapeDtypeStruct((EXTRA, COV), F32),
        ),
        in_specs=[hbm] * 5,
        out_specs=(vmem, vmem, vmem),
        scratch_shapes=[
            pltpu.SMEM((SAMP,), jnp.int32),
            pltpu.VMEM((ROWS, COV), BF16),
            pltpu.VMEM((1, ROWS), jnp.int32),
            pltpu.VMEM((1, ROWS), jnp.int32),
            pltpu.VMEM((1, ROWS), F32),
            pltpu.VMEM((8, LANES), jnp.int32),
            pltpu.VMEM((GROUP, 8, LANES), jnp.int32),
            pltpu.VMEM((2 * 64, ROWS), BF16),
            pltpu.VMEM((COLS, ROWS), BF16),
            pltpu.VMEM((GROUP, SAMP, COLS), BF16),
            pltpu.VMEM((GROUP, SAMP, COLS), BF16),
            pltpu.VMEM((NZ, SAMP, COLS), BF16),
            pltpu.VMEM((2, COV + EXTRA, COV), F32),
            pltpu.VMEM((COV + EXTRA, COV), F32),
            pltpu.VMEM((NZ, 16 + EXTRA, COV), F32),
            pltpu.VMEM((NZ, 16 + EXTRA, COV), F32),
            pltpu.VMEM((NX, 16 + EXTRA, COV), F32),
            pltpu.VMEM((NY, 16 + EXTRA, COV), F32),
            pltpu.SemaphoreType.DMA((N_COPIES,)),
            pltpu.SemaphoreType.DMA((N_COPIES,)),
            pltpu.SemaphoreType.DMA((5,)),
        ],
        compiler_params=pltpu.CompilerParams(
            collective_id=0, has_side_effects=True, vmem_limit_bytes=40 << 20
        ),
        name="gather_sketch",
    )(samples, covariates, codes, bits, noise)


def column(value, index):
    return jnp.broadcast_to(value[:, index : index + 1], value.shape)


def six(value, order, axis):
    parts = split3(value)
    return jnp.concatenate([parts[i] for i in order], axis=axis).astype(BF16)


def product6(left, right, turned=False):
    axis = 0 if turned else 1
    return lax.dot_general(
        six(left, (0, 0, 0, 1, 1, 2), axis), six(right, (0, 1, 2, 0, 1, 0), 0),
        (((axis,), (0,)), ((), ())), preferred_element_type=F32,
    )


AHEAD = 4
PANEL = 8
SLOTS = 2 * PANEL + 1


def invert_factor(matrix, slots):
    count = COV // PANEL
    shape = (PANEL, COV)
    rows = [matrix[PANEL * t : PANEL * (t + 1), :] for t in range(count)]
    sub = iota(shape, 0)
    lane = iota(shape, 1)

    def columns(t, first):
        return [column(rows[t], first + i) for i in range(PANEL)]

    def spread(slot, index):
        return slots[slot, pl.ds(index, PANEL, stride=0), :]

    pivot = columns(0, 0)
    for p in range(count):
        base = (p % 2) * SLOTS
        first = PANEL * p
        panel = (lane >= first) & (lane < first + PANEL)
        near = range(p + 1, min(p + 1 + AHEAD, count))
        far = range(min(p + 1 + AHEAD, count), count)
        own = {t: columns(t, first) for t in near}
        after = columns(p + 1, first + PANEL) if p + 1 < count else None
        for c in range(PANEL):
            slots[base + c] = pivot[c]
        left = [[spread(base + c, a) for c in range(a + 1)] for a in range(PANEL)]
        rows[p] = jnp.where(panel, jnp.where(lane == first + sub, 1.0, 0.0), rows[p])
        slots[base + PANEL] = rows[p]
        start = [spread(base + PANEL, i) for i in range(PANEL)]
        root = []
        low = [[None] * PANEL for _ in range(PANEL)]
        for i in range(PANEL):
            root.append(lax.rsqrt(left[i][i]))
            for a in range(i + 1, PANEL):
                low[a][i] = left[a][i] * root[i]
            for a in range(i + 1, PANEL):
                for c in range(i + 1, a + 1):
                    left[a][c] = left[a][c] - low[a][i] * low[c][i]

        def multipliers(t):
            scales = []
            for i in range(PANEL):
                scale = own[t][i]
                for k in range(i):
                    scale = scale - scales[k] * low[i][k]
                scales.append(scale * root[i])
            return scales

        scales = {}
        if after:
            scales[p + 1] = multipliers(p + 1)
            for i, scale in enumerate(scales[p + 1]):
                slot = base + PANEL + 1 + i
                slots[slot] = scale
                for c in range(PANEL):
                    after[c] = after[c] - scale * spread(slot, c)
            pivot = after
        row = []
        for i in range(PANEL):
            value = start[i]
            for k in range(i):
                value = value - low[i][k] * row[k]
            row.append(value * root[i])
        value = row[PANEL - 1]
        for i in range(PANEL - 1):
            value = jnp.where(sub == i, row[i], value)
        rows[p] = value
        if len(far):
            change = product6(value, value, turned=True)
        for t in near:
            if t not in scales:
                scales[t] = multipliers(t)
            value = jnp.where(panel, 0.0, rows[t])
            for scale, one in zip(scales[t], row):
                value = value - scale * one
            rows[t] = value
        for t in far:
            rows[t] = jnp.where(panel, 0.0, rows[t]) - change[PANEL * t : PANEL * (t + 1), :]
    for p in range(count):
        rows[p] = jnp.where(lane <= PANEL * p + sub, rows[p], 0.0)
    return jnp.concatenate(rows, axis=0)


def blk(index):
    return slice(index * COV, (index + 1) * COV)


def solve_kernel(
    sketch_ref, square_ref, extra_ref, effects_hbm, cov_hbm, codes_hbm, noise_hbm,
    coef_ref, resid_ref, factor_hbm, gram, inverse,
    factor_ref, effects_ref, cov_ref, codes_ref, noise_ref, slots, load, store,
):
    loads = [
        pltpu.make_async_copy(src, dst, load.at[i])
        for i, (src, dst) in enumerate(
            [
                (effects_hbm, effects_ref), (cov_hbm, cov_ref), (codes_hbm, codes_ref),
                (noise_hbm, noise_ref),
            ]
        )
    ]
    for copy in loads:
        copy.start()
    stores = []
    n = LEVELS
    sub = iota((COV, COV), 0)
    lane = iota((COV, COV), 1)
    scale = math.sqrt(LEVELS / SKETCH)
    for k in range(n):
        gram[k, :, k * COV :] = lax.dot_general(
            sketch_ref[:, blk(k)], sketch_ref[:, k * COV :], (((0,), (0,)), ((), ())),
            preferred_element_type=F32,
        )
    matrix = gram[0, :, blk(0)]
    for k in range(n):
        current = matrix
        corner = invert_factor(current, slots)
        inverse[k, :, blk(k)] = corner
        head = None
        if k + 1 < n:
            head = product6(corner, gram[k, :, blk(k + 1)])
            matrix = gram[k + 1, :, blk(k + 1)] - product6(head, head, turned=True)
        if k:
            inverse[k, :, : k * COV] = product6(corner, gram[k, :, : k * COV])
            factor_ref[blk(k), : k * COV] = jnp.zeros((COV, k * COV), F32)
        own = product6(corner, current)
        factor_ref[blk(k), blk(k)] = jnp.where(lane >= sub, own, 0.0) * scale
        upper = {k + 1: head}
        if k + 1 < n:
            factor_ref[blk(k), blk(k + 1)] = head * scale
        if k + 2 < n:
            rest = product6(corner, gram[k, :, (k + 2) * COV :])
            factor_ref[blk(k), (k + 2) * COV :] = rest * scale
            for i in range(k + 2, n):
                upper[i] = rest[:, blk(i - k - 2)]
        part = pltpu.make_async_copy(factor_ref.at[blk(k)], factor_hbm.at[blk(k)], store.at[k])
        part.start()
        stores.append(part)
        for i in range(k + 1, n):
            for j in range(i, n):
                if j > k + 1:
                    change = product6(upper[i], upper[j], turned=True)
                    gram[i, :, blk(j)] = gram[i, :, blk(j)] - change
            change = product6(upper[i], inverse[k, :, : (k + 1) * COV], turned=True)
            if k:
                gram[i, :, : k * COV] = gram[i, :, : k * COV] - change[:, : k * COV]
            gram[i, :, blk(k)] = -change[:, blk(k)]

    normal = []
    for pair in range(2):
        square = square_ref[pair]
        turned = square.T
        diagonal = extra_ref[4 + pair : 5 + pair, :]
        normal.append(jnp.where(lane >= sub, square, turned))
        normal.append(jnp.where(lane < sub, square, jnp.where(lane > sub, turned, diagonal)))

    def apply_normal(rows):
        out = []
        for level in range(n):
            column = jnp.sum(normal[level] * rows[level], axis=1, keepdims=True)
            out.append(jnp.sum(jnp.where(lane == sub, column, 0.0), axis=0, keepdims=True))
        return out

    def forward(rows):
        out = []
        for k in range(n):
            acc = inverse[k, :, blk(0)] * rows[0]
            for c in range(1, k + 1):
                acc = acc + inverse[k, :, blk(c)] * rows[c]
            out.append(jnp.sum(acc, axis=1, keepdims=True))
        return out

    def backward(columns):
        out = []
        for c in range(n):
            acc = inverse[c, :, blk(c)] * columns[c]
            for k in range(c + 1, n):
                acc = acc + inverse[k, :, blk(c)] * columns[k]
            out.append(jnp.sum(acc, axis=0, keepdims=True))
        return out

    def dot(left, right, axis):
        acc = left[0] * right[0]
        for a, b in zip(left[1:], right[1:]):
            acc = acc + a * b
        return jnp.sum(acc, axis=axis, keepdims=True)

    for copy in loads:
        copy.wait()
    effects = [effects_ref[:, blk(level)] for level in range(n)]
    gradient = [
        image + extra_ref[level : level + 1, :] for level, image in enumerate(apply_normal(effects))
    ]
    steer = forward(gradient)
    gamma = dot(steer, steer, 0)
    direction = backward(steer)
    solved = [jnp.zeros((1, COV), F32)] * n
    for step in range(ITERS):
        image = apply_normal(direction)
        alpha = gamma / dot(direction, image, 1)
        solved = [a + alpha * b for a, b in zip(solved, direction)]
        if step + 1 < ITERS:
            gradient = [a - alpha * b for a, b in zip(gradient, image)]
            steer = forward(gradient)
            gamma_new = dot(steer, steer, 0)
            ratio = gamma_new / gamma
            direction = [a + ratio * b for a, b in zip(backward(steer), direction)]
            gamma = gamma_new
    left = []
    for level in range(n):
        coef_ref[:, blk(level)] = solved[level]
        left.append(effects[level] - solved[level])
    parts = split3(jnp.concatenate(left, axis=0))
    weights = jnp.concatenate(list(parts) + [jnp.zeros((4, COV), F32)], axis=0).astype(BF16)
    values = lax.dot_general(
        weights, cov_ref[...], (((1,), (1,)), ((), ())), preferred_element_type=F32
    )
    codes = codes_ref[...]
    resid = noise_ref[...]
    for level in range(n):
        value = values[level : level + 1] + values[4 + level : 5 + level] + values[8 + level : 9 + level]
        resid = resid + jnp.where(codes == level, value, 0.0)
    resid_ref[...] = resid
    for copy in stores:
        copy.wait()


def solve(sketch, square, extra, effects, covariates, codes, noise):
    vmem = pl.BlockSpec(memory_space=pltpu.VMEM)
    hbm = pl.BlockSpec(memory_space=pltpu.HBM)
    return pl.pallas_call(
        solve_kernel,
        out_shape=(
            jax.ShapeDtypeStruct((1, COLS), F32),
            jax.ShapeDtypeStruct((1, ROWS), F32),
            jax.ShapeDtypeStruct((COLS, COLS), F32),
        ),
        in_specs=[vmem] * 3 + [hbm] * 4,
        out_specs=(vmem, vmem, hbm),
        scratch_shapes=[
            pltpu.VMEM((LEVELS, COV, COLS), F32),
            pltpu.VMEM((LEVELS, COV, COLS), F32),
            pltpu.VMEM((COLS, COLS), F32),
            pltpu.VMEM((1, COLS), F32),
            pltpu.VMEM((ROWS, COV), BF16),
            pltpu.VMEM((1, ROWS), jnp.int32),
            pltpu.VMEM((1, ROWS), F32),
            pltpu.VMEM((2 * SLOTS, PANEL, COV), F32),
            pltpu.SemaphoreType.DMA((4,)),
            pltpu.SemaphoreType.DMA((LEVELS,)),
        ],
        compiler_params=pltpu.CompilerParams(vmem_limit_bytes=40 << 20),
        name="solve",
    )(sketch, square, extra, effects, covariates, codes, noise)


def body(covariates, level_codes, sign_bits, sample_rows, effects, noise):
    def fixed(value):
        return pltpu.with_memory_space_constraint(value, pltpu.HBM)

    covariates = fixed(covariates)
    codes = fixed(level_codes.reshape(1, ROWS))
    noise = fixed(noise.reshape(1, ROWS))
    sketch, square, extra = gather(
        fixed(sample_rows), covariates, codes, fixed(sign_bits.reshape(1, ROWS)), noise
    )
    coef, resid, factor = solve(
        sketch.reshape(SKETCH, COLS), square.reshape(2, COV, COV), extra,
        fixed(effects.reshape(1, COLS)), covariates, codes, noise,
    )
    return coef.reshape(COLS), resid.reshape(ROWS), factor


def solution(mesh):
    rows = P(("wide", "narrow"))
    return jax.shard_map(
        body,
        mesh=mesh,
        in_specs=(P(("wide", "narrow"), None), rows, rows, rows, P(), rows),
        out_specs=(P(), rows, P()),
        check_vma=False,
    )
```

```python
import functools
import math

import jax
import jax.numpy as jnp
from jax import lax
from jax.experimental import pallas as pl
from jax.experimental.pallas import tpu as pltpu
from jax.sharding import PartitionSpec as P

COV = 128
LEVELS = 4
COLS = COV * LEVELS
ROWS = 2048
HB = 256
SKETCH = 1024
SAMP = 4
ITERS = 4
GROUP = 8
NZ = 8
NX = 4
NY = 4
EXTRA = 8
LANES = 128

HALF_ROOT = math.sqrt(0.5)
HIGH = lax.Precision.HIGHEST
MESH = pl.DeviceIdType.MESH
F32 = jnp.float32
BF16 = jnp.bfloat16


def iota(shape, axis):
    return lax.broadcasted_iota(jnp.int32, shape, axis)


def split3(value):
    high = value.astype(BF16)
    rest = value - high.astype(F32)
    middle = rest.astype(BF16)
    low = (rest - middle.astype(F32)).astype(BF16)
    return high.astype(F32), middle.astype(F32), low.astype(F32)


def ring(offset, size):
    return min(offset, size - offset)


Z_FAR = sorted(range(1, NZ), key=lambda o: -ring(o, NZ))
FOUR_FAR = (2, 1, 3)
MIX_FAR = sorted(
    [(dx, dc) for dx in range(4) for dc in range(2) if (dx, dc) != (0, 0)],
    key=lambda o: -(ring(o[0], 4) + o[1]),
)


def gather_kernel(
    samp_hbm, cov_hbm, codes_hbm, bits_hbm, noise_hbm,
    sketch_ref, square_ref, extra_ref,
    samp_ref, cov_ref, codes_ref, bits_ref, noise_ref,
    own, asked, picks, lhs, sent, held, rowz,
    halves, half_in, pieces, piece_in, row_in, col_in,
    send, recv, load,
):
    loads = [
        pltpu.make_async_copy(src, dst, load.at[i])
        for i, (src, dst) in enumerate(
            [
                (samp_hbm, samp_ref), (cov_hbm, cov_ref), (codes_hbm, codes_ref),
                (bits_hbm, bits_ref), (noise_hbm, noise_ref),
            ]
        )
    ]
    for copy in loads:
        copy.start()
    wide = lax.axis_index("wide")
    z = lax.axis_index("narrow")
    core = lax.rem(wide, 2)
    q = wide // 2
    x = lax.rem(q, 4)
    y = q // 4
    member = lax.rem(wide, GROUP)
    base = wide - member
    sibling = wide + 1 - 2 * core
    mix_peers = [lax.rem(x + dx, 4) * 2 + lax.rem(core + dc, 2) for dx, dc in MIX_FAR]
    z_peers = [lax.rem(z + o, NZ) for o in Z_FAR]
    x_peers = [(y * 4 + lax.rem(x + o, 4)) * 2 + core for o in FOUR_FAR]
    y_peers = [(lax.rem(y + o, 4) * 4 + x) * 2 + core for o in FOUR_FAR]

    slots = iter(range(N_COPIES))

    def remote(src, dst, to_wide, to_z):
        slot = next(slots)
        return pltpu.make_async_remote_copy(
            src_ref=src, dst_ref=dst, send_sem=send.at[slot], recv_sem=recv.at[slot],
            device_id=(to_wide, to_z), device_id_type=MESH,
        )

    barrier = pltpu.get_barrier_semaphore()
    for peer in z_peers:
        pl.semaphore_signal(barrier, inc=1, device_id=(wide, peer), device_id_type=MESH)
    for peer in y_peers:
        pl.semaphore_signal(barrier, inc=1, device_id=(peer, z), device_id_type=MESH)
    for peer in mix_peers:
        pl.semaphore_signal(barrier, inc=1, device_id=(base + peer, z), device_id_type=MESH)

    for copy in loads[1:]:
        copy.wait()
    codes = codes_ref[...]
    flip = cov_ref[...].astype(F32).T
    masks = [(codes == level).astype(F32) for level in range(LEVELS)]
    for level in range(LEVELS):
        lhs[level * COV : (level + 1) * COV, :] = (flip * masks[level]).astype(BF16)
    parts = split3(noise_ref[...])
    shadow_rows = [part * mask for part in parts for mask in masks]
    shadow_rows = jnp.concatenate(shadow_rows + [jnp.zeros((4, ROWS), F32)], axis=0)
    normal = jnp.dot(lhs[...], cov_ref[...], preferred_element_type=F32)
    shadow = jnp.dot(shadow_rows.astype(BF16), cov_ref[...], preferred_element_type=F32)
    shadow = shadow[0:4] + shadow[4:8] + shadow[8:12]
    sub = iota((COV, COV), 0)
    lane = iota((COV, COV), 1)
    diagonals = []
    for pair in range(2):
        even = normal[2 * pair * COV : (2 * pair + 1) * COV]
        odd = normal[(2 * pair + 1) * COV : (2 * pair + 2) * COV]
        halves[pair, 0:COV, :] = jnp.where(lane >= sub, even, odd)
        diagonals.append(jnp.sum(jnp.where(lane == sub, odd, 0.0), axis=0, keepdims=True))
    extra = jnp.concatenate([shadow] + diagonals + [jnp.zeros((2, COV), F32)], axis=0)
    halves[0, COV:, :] = extra
    halves[1, COV:, :] = extra
    loads[0].wait()
    for k in range(8):
        own[k : k + 1, :] = jnp.full((1, LANES), samp_ref[k % SAMP], jnp.int32)
    asked[member] = own[...]
    pl.semaphore_wait(barrier, len(Z_FAR) + len(FOUR_FAR) + len(MIX_FAR))

    ask = [remote(own, asked.at[member], base + peer, z) for peer in mix_peers]
    for copy in ask:
        copy.start()

    a_core = remote(halves.at[1 - core], half_in, sibling, z)
    a_core.start()

    a_core.wait_recv()
    mine = halves[core] + half_in[...]
    for i in range(NZ):
        pieces[i] = jnp.concatenate([mine[i * 16 : (i + 1) * 16], mine[COV:]], axis=0)
    piece_in[z] = pieces[z]
    a_z = [remote(pieces.at[peer], piece_in.at[z], wide, peer) for peer in z_peers]
    for copy in a_z:
        copy.start()

    for copy in ask:
        copy.wait_recv()
    want = jnp.concatenate([asked[i] for i in range(GROUP)], axis=0)
    shape = (GROUP * 8, LANES)
    common = want & iota(shape, 1)
    common = common ^ (common >> 4)
    common = common ^ (common >> 2)
    low = common ^ (common >> 1)
    top = (want >> 7) & 1
    block = want >> 8
    upper_half = (iota(shape, 0) // SAMP) & 1
    for chunk in range(ROWS // LANES):
        span = slice(chunk * LANES, (chunk + 1) * LANES)
        parity = low ^ bits_ref[:, span]
        if chunk % 2:
            parity = parity ^ top
        sign = (1 - 2 * (parity & 1)).astype(F32)
        sign = jnp.where(block == chunk // 2, sign, 0.0)
        here = codes_ref[:, span]
        for pair in range(2):
            value = jnp.where(here == 2 * pair + upper_half, sign, 0.0)
            picks[pair * 64 : (pair + 1) * 64, span] = value.astype(BF16)
    local = jnp.dot(picks[...], cov_ref[...], preferred_element_type=F32)
    local = local * (1.0 / math.sqrt(HB))
    for i in range(GROUP):
        spots = [pair * 64 + i * 8 + SAMP * half for pair in range(2) for half in range(2)]
        sent[i] = jnp.concatenate([local[at : at + SAMP] for at in spots], axis=1).astype(BF16)
    held[member] = sent[member]
    rows = [remote(sent.at[peer], held.at[member], base + peer, z) for peer in mix_peers]
    for copy in rows:
        copy.start()

    for copy in a_z:
        copy.wait_recv()
    total = piece_in[0]
    for i in range(1, NZ):
        total = total + piece_in[i]
    row_in[x] = total
    a_x = [remote(row_in.at[x], row_in.at[x], peer, z) for peer in x_peers]
    for copy in a_x:
        copy.start()

    for copy in rows:
        copy.wait_recv()
    level_rows = [held[i].astype(F32) for i in range(GROUP)]
    for place in range(3):
        side = (1 - 2 * lax.rem(wide // (2**place), 2)).astype(F32)
        level_rows = [
            ((level_rows[i] + side * level_rows[i + 1]) * HALF_ROOT).astype(BF16).astype(F32)
            for i in range(0, len(level_rows), 2)
        ]
    rowz[z] = level_rows[0].astype(BF16)
    s_z = [remote(rowz.at[z], rowz.at[z], wide, peer) for peer in z_peers]
    for copy in s_z:
        copy.start()

    for copy in a_x:
        copy.wait_recv()
    total = row_in[0]
    for i in range(1, NX):
        total = total + row_in[i]
    col_in[y] = total
    a_y = [remote(col_in.at[y], col_in.at[y], peer, z) for peer in y_peers]
    for copy in a_y:
        copy.start()

    for copy in s_z:
        copy.wait_recv()
    stack = jnp.concatenate([rowz[i].astype(F32) for i in range(NZ)], axis=0).astype(BF16)
    sketch_ref[0, core, y, x] = stack[:16]
    sketch_ref[1, core, x, y] = stack[16:]
    first = sketch_ref.at[0, core, y, x]
    second = sketch_ref.at[1, core, x, y]
    s_first = [remote(first, first, peer, z) for peer in x_peers]
    s_second = [remote(second, second, peer, z) for peer in y_peers]
    for one, two in zip(s_first, s_second):
        one.start()
        two.start()
    s_line = [[] for _ in FOUR_FAR]
    s_other = [[] for _ in FOUR_FAR]

    def along(x_from, y_from):
        line = sketch_ref.at[0, core, y, x_from]
        other = sketch_ref.at[1, core, x, y_from]
        for i in range(len(FOUR_FAR)):
            s_line[i].append(remote(line, line, y_peers[i], z))
            s_other[i].append(remote(other, other, x_peers[i], z))
            s_line[i][-1].start()
            s_other[i][-1].start()

    along(x, y)

    for copy in a_y:
        copy.wait_recv()
    total = col_in[0]
    for i in range(1, NY):
        total = total + col_in[i]
    extra_ref[...] = total[16:]
    square_ref[core, z] = total[:16]
    mine = square_ref.at[core, z]
    a_out = [remote(mine, mine, wide, peer) for peer in z_peers]
    for copy in a_out:
        copy.start()

    for i in (2, 1, 0):
        s_first[i].wait_recv()
        s_second[i].wait_recv()
        along(lax.rem(x - FOUR_FAR[i] + 4, 4), lax.rem(y - FOUR_FAR[i] + 4, 4))
    line = sketch_ref.at[0, core, y]
    other = sketch_ref.at[1, core, x]
    s_core = [remote(line, line, sibling, z), remote(other, other, sibling, z)]
    for copy in s_core:
        copy.start()

    def onward(index):
        for copy in s_line[index]:
            copy.wait_recv()
        passed = sketch_ref.at[0, core, lax.rem(y - FOUR_FAR[index] + 4, 4)]
        copy = remote(passed, passed, sibling, z)
        copy.start()
        s_core.append(copy)
        for copy in s_other[index]:
            copy.wait_recv()
        passed = sketch_ref.at[1, core, lax.rem(x - FOUR_FAR[index] + 4, 4)]
        copy = remote(passed, passed, sibling, z)
        copy.start()
        s_core.append(copy)

    onward(1)
    onward(2)
    for copy in a_out:
        copy.wait_recv()
    a_last = remote(square_ref.at[core], square_ref.at[core], sibling, z)
    a_last.start()
    onward(0)
    a_last.wait_recv()
    for copy in s_core:
        copy.wait_recv()
    sums = [a_core] + a_z + a_x + a_y + a_out + [a_last]
    lines = [copy for group in s_line + s_other for copy in group]
    for copy in ask + rows + s_z + s_first + s_second + lines + s_core + sums:
        copy.wait_send()


N_COPIES = 7 + 1 + 7 + 7 + 7 + 3 + 6 + 3 + 24 + 8 + 7 + 1


def gather(samples, covariates, codes, bits, noise):
    vmem = pl.BlockSpec(memory_space=pltpu.VMEM)
    hbm = pl.BlockSpec(memory_space=pltpu.HBM)
    return pl.pallas_call(
        gather_kernel,
        out_shape=(
            jax.ShapeDtypeStruct((2, 2, 4, 4, 16, COLS), BF16),
            jax.ShapeDtypeStruct((2, NZ, 16, COV), F32),
            jax.ShapeDtypeStruct((EXTRA, COV), F32),
        ),
        in_specs=[hbm] * 5,
        out_specs=(vmem, vmem, vmem),
        scratch_shapes=[
            pltpu.SMEM((SAMP,), jnp.int32),
            pltpu.VMEM((ROWS, COV), BF16),
            pltpu.VMEM((1, ROWS), jnp.int32),
            pltpu.VMEM((1, ROWS), jnp.int32),
            pltpu.VMEM((1, ROWS), F32),
            pltpu.VMEM((8, LANES), jnp.int32),
            pltpu.VMEM((GROUP, 8, LANES), jnp.int32),
            pltpu.VMEM((2 * 64, ROWS), BF16),
            pltpu.VMEM((COLS, ROWS), BF16),
            pltpu.VMEM((GROUP, SAMP, COLS), BF16),
            pltpu.VMEM((GROUP, SAMP, COLS), BF16),
            pltpu.VMEM((NZ, SAMP, COLS), BF16),
            pltpu.VMEM((2, COV + EXTRA, COV), F32),
            pltpu.VMEM((COV + EXTRA, COV), F32),
            pltpu.VMEM((NZ, 16 + EXTRA, COV), F32),
            pltpu.VMEM((NZ, 16 + EXTRA, COV), F32),
            pltpu.VMEM((NX, 16 + EXTRA, COV), F32),
            pltpu.VMEM((NY, 16 + EXTRA, COV), F32),
            pltpu.SemaphoreType.DMA((N_COPIES,)),
            pltpu.SemaphoreType.DMA((N_COPIES,)),
            pltpu.SemaphoreType.DMA((5,)),
        ],
        compiler_params=pltpu.CompilerParams(
            collective_id=0, has_side_effects=True, vmem_limit_bytes=40 << 20
        ),
        name="gather_sketch",
    )(samples, covariates, codes, bits, noise)


def column(value, index):
    return jnp.broadcast_to(value[:, index : index + 1], value.shape)


def six(value, order, axis):
    parts = split3(value)
    return jnp.concatenate([parts[i] for i in order], axis=axis).astype(BF16)


def product6(left, right, turned=False):
    axis = 0 if turned else 1
    return lax.dot_general(
        six(left, (0, 0, 0, 1, 1, 2), axis), six(right, (0, 1, 2, 0, 1, 0), 0),
        (((axis,), (0,)), ((), ())), preferred_element_type=F32,
    )


AHEAD = 4
PANEL = 8
SLOTS = 2 * PANEL + 1


def invert_factor(matrix, slots):
    count = COV // PANEL
    shape = (PANEL, COV)
    rows = [matrix[PANEL * t : PANEL * (t + 1), :] for t in range(count)]
    sub = iota(shape, 0)
    lane = iota(shape, 1)

    def columns(t, first):
        return [column(rows[t], first + i) for i in range(PANEL)]

    def spread(slot, index):
        return slots[slot, pl.ds(index, PANEL, stride=0), :]

    pivot = columns(0, 0)
    for p in range(count):
        base = (p % 2) * SLOTS
        first = PANEL * p
        panel = (lane >= first) & (lane < first + PANEL)
        near = range(p + 1, min(p + 1 + AHEAD, count))
        far = range(min(p + 1 + AHEAD, count), count)
        own = {t: columns(t, first) for t in near}
        after = columns(p + 1, first + PANEL) if p + 1 < count else None
        for c in range(PANEL):
            slots[base + c] = pivot[c]
        left = [[spread(base + c, a) for c in range(a + 1)] for a in range(PANEL)]
        rows[p] = jnp.where(panel, jnp.where(lane == first + sub, 1.0, 0.0), rows[p])
        slots[base + PANEL] = rows[p]
        start = [spread(base + PANEL, i) for i in range(PANEL)]
        root = []
        low = [[None] * PANEL for _ in range(PANEL)]
        for i in range(PANEL):
            root.append(lax.rsqrt(left[i][i]))
            for a in range(i + 1, PANEL):
                low[a][i] = left[a][i] * root[i]
            for a in range(i + 1, PANEL):
                for c in range(i + 1, a + 1):
                    left[a][c] = left[a][c] - low[a][i] * low[c][i]

        def multipliers(t):
            scales = []
            for i in range(PANEL):
                scale = own[t][i]
                for k in range(i):
                    scale = scale - scales[k] * low[i][k]
                scales.append(scale * root[i])
            return scales

        scales = {}
        if after:
            scales[p + 1] = multipliers(p + 1)
            for i, scale in enumerate(scales[p + 1]):
                slot = base + PANEL + 1 + i
                slots[slot] = scale
                for c in range(PANEL):
                    after[c] = after[c] - scale * spread(slot, c)
            pivot = after
        row = []
        for i in range(PANEL):
            value = start[i]
            for k in range(i):
                value = value - low[i][k] * row[k]
            row.append(value * root[i])
        value = row[PANEL - 1]
        for i in range(PANEL - 1):
            value = jnp.where(sub == i, row[i], value)
        rows[p] = value
        if len(far):
            change = product6(value, value, turned=True)
        for t in near:
            if t not in scales:
                scales[t] = multipliers(t)
            value = jnp.where(panel, 0.0, rows[t])
            for scale, one in zip(scales[t], row):
                value = value - scale * one
            rows[t] = value
        for t in far:
            rows[t] = jnp.where(panel, 0.0, rows[t]) - change[PANEL * t : PANEL * (t + 1), :]
    for p in range(count):
        rows[p] = jnp.where(lane <= PANEL * p + sub, rows[p], 0.0)
    return jnp.concatenate(rows, axis=0)


def blk(index):
    return slice(index * COV, (index + 1) * COV)


def solve_kernel(
    sketch_ref, square_ref, extra_ref, effects_hbm, cov_hbm, codes_hbm, noise_hbm,
    coef_ref, resid_ref, factor_hbm, gram, inverse,
    factor_ref, effects_ref, cov_ref, codes_ref, noise_ref, slots, load, store,
):
    loads = [
        pltpu.make_async_copy(src, dst, load.at[i])
        for i, (src, dst) in enumerate(
            [
                (effects_hbm, effects_ref), (cov_hbm, cov_ref), (codes_hbm, codes_ref),
                (noise_hbm, noise_ref),
            ]
        )
    ]
    for copy in loads:
        copy.start()
    stores = []
    n = LEVELS
    sub = iota((COV, COV), 0)
    lane = iota((COV, COV), 1)
    scale = math.sqrt(LEVELS / SKETCH)
    for k in range(n):
        gram[k, :, k * COV :] = lax.dot_general(
            sketch_ref[:, blk(k)], sketch_ref[:, k * COV :], (((0,), (0,)), ((), ())),
            preferred_element_type=F32,
        )
    matrix = gram[0, :, blk(0)]
    for k in range(n):
        current = matrix
        corner = invert_factor(current, slots)
        inverse[k, :, blk(k)] = corner
        head = None
        if k + 1 < n:
            head = product6(corner, gram[k, :, blk(k + 1)])
            matrix = gram[k + 1, :, blk(k + 1)] - product6(head, head, turned=True)
        if k:
            inverse[k, :, : k * COV] = product6(corner, gram[k, :, : k * COV])
            factor_ref[blk(k), : k * COV] = jnp.zeros((COV, k * COV), F32)
        own = product6(corner, current)
        factor_ref[blk(k), blk(k)] = jnp.where(lane >= sub, own, 0.0) * scale
        upper = {k + 1: head}
        if k + 1 < n:
            factor_ref[blk(k), blk(k + 1)] = head * scale
        if k + 2 < n:
            rest = product6(corner, gram[k, :, (k + 2) * COV :])
            factor_ref[blk(k), (k + 2) * COV :] = rest * scale
            for i in range(k + 2, n):
                upper[i] = rest[:, blk(i - k - 2)]
        part = pltpu.make_async_copy(factor_ref.at[blk(k)], factor_hbm.at[blk(k)], store.at[k])
        part.start()
        stores.append(part)
        for i in range(k + 1, n):
            for j in range(i, n):
                if j > k + 1:
                    change = product6(upper[i], upper[j], turned=True)
                    gram[i, :, blk(j)] = gram[i, :, blk(j)] - change
            change = product6(upper[i], inverse[k, :, : (k + 1) * COV], turned=True)
            if k:
                gram[i, :, : k * COV] = gram[i, :, : k * COV] - change[:, : k * COV]
            gram[i, :, blk(k)] = -change[:, blk(k)]

    normal = []
    for pair in range(2):
        square = square_ref[pair]
        turned = square.T
        diagonal = extra_ref[4 + pair : 5 + pair, :]
        normal.append(jnp.where(lane >= sub, square, turned))
        normal.append(jnp.where(lane < sub, square, jnp.where(lane > sub, turned, diagonal)))

    def apply_normal(rows):
        out = []
        for level in range(n):
            column = jnp.sum(normal[level] * rows[level], axis=1, keepdims=True)
            out.append(jnp.sum(jnp.where(lane == sub, column, 0.0), axis=0, keepdims=True))
        return out

    def forward(rows):
        out = []
        for k in range(n):
            acc = inverse[k, :, blk(0)] * rows[0]
            for c in range(1, k + 1):
                acc = acc + inverse[k, :, blk(c)] * rows[c]
            out.append(jnp.sum(acc, axis=1, keepdims=True))
        return out

    def backward(columns):
        out = []
        for c in range(n):
            acc = inverse[c, :, blk(c)] * columns[c]
            for k in range(c + 1, n):
                acc = acc + inverse[k, :, blk(c)] * columns[k]
            out.append(jnp.sum(acc, axis=0, keepdims=True))
        return out

    def dot(left, right, axis):
        acc = left[0] * right[0]
        for a, b in zip(left[1:], right[1:]):
            acc = acc + a * b
        return jnp.sum(acc, axis=axis, keepdims=True)

    for copy in loads:
        copy.wait()
    effects = [effects_ref[:, blk(level)] for level in range(n)]
    gradient = [
        image + extra_ref[level : level + 1, :] for level, image in enumerate(apply_normal(effects))
    ]
    steer = forward(gradient)
    gamma = dot(steer, steer, 0)
    direction = backward(steer)
    solved = [jnp.zeros((1, COV), F32)] * n
    for step in range(ITERS):
        image = apply_normal(direction)
        alpha = gamma / dot(direction, image, 1)
        solved = [a + alpha * b for a, b in zip(solved, direction)]
        if step + 1 < ITERS:
            gradient = [a - alpha * b for a, b in zip(gradient, image)]
            steer = forward(gradient)
            gamma_new = dot(steer, steer, 0)
            ratio = gamma_new / gamma
            direction = [a + ratio * b for a, b in zip(backward(steer), direction)]
            gamma = gamma_new
    left = []
    for level in range(n):
        coef_ref[:, blk(level)] = solved[level]
        left.append(effects[level] - solved[level])
    parts = split3(jnp.concatenate(left, axis=0))
    weights = jnp.concatenate(list(parts) + [jnp.zeros((4, COV), F32)], axis=0).astype(BF16)
    values = lax.dot_general(
        weights, cov_ref[...], (((1,), (1,)), ((), ())), preferred_element_type=F32
    )
    codes = codes_ref[...]
    resid = noise_ref[...]
    for level in range(n):
        value = values[level : level + 1] + values[4 + level : 5 + level] + values[8 + level : 9 + level]
        resid = resid + jnp.where(codes == level, value, 0.0)
    resid_ref[...] = resid
    for copy in stores:
        copy.wait()


def solve(sketch, square, extra, effects, covariates, codes, noise):
    vmem = pl.BlockSpec(memory_space=pltpu.VMEM)
    hbm = pl.BlockSpec(memory_space=pltpu.HBM)
    return pl.pallas_call(
        solve_kernel,
        out_shape=(
            jax.ShapeDtypeStruct((1, COLS), F32),
            jax.ShapeDtypeStruct((1, ROWS), F32),
            jax.ShapeDtypeStruct((COLS, COLS), F32),
        ),
        in_specs=[vmem] * 3 + [hbm] * 4,
        out_specs=(vmem, vmem, hbm),
        scratch_shapes=[
            pltpu.VMEM((LEVELS, COV, COLS), F32),
            pltpu.VMEM((LEVELS, COV, COLS), F32),
            pltpu.VMEM((COLS, COLS), F32),
            pltpu.VMEM((1, COLS), F32),
            pltpu.VMEM((ROWS, COV), BF16),
            pltpu.VMEM((1, ROWS), jnp.int32),
            pltpu.VMEM((1, ROWS), F32),
            pltpu.VMEM((2 * SLOTS, PANEL, COV), F32),
            pltpu.SemaphoreType.DMA((4,)),
            pltpu.SemaphoreType.DMA((LEVELS,)),
        ],
        compiler_params=pltpu.CompilerParams(vmem_limit_bytes=40 << 20),
        name="solve",
    )(sketch, square, extra, effects, covariates, codes, noise)


def body(covariates, level_codes, sign_bits, sample_rows, effects, noise):
    def fixed(value):
        return pltpu.with_memory_space_constraint(value, pltpu.HBM)

    covariates = fixed(covariates)
    codes = fixed(level_codes.reshape(1, ROWS))
    noise = fixed(noise.reshape(1, ROWS))
    sketch, square, extra = gather(
        fixed(sample_rows), covariates, codes, fixed(sign_bits.reshape(1, ROWS)), noise
    )
    coef, resid, factor = solve(
        sketch.reshape(SKETCH, COLS), square.reshape(2, COV, COV), extra,
        fixed(effects.reshape(1, COLS)), covariates, codes, noise,
    )
    return coef.reshape(COLS), resid.reshape(ROWS), factor


def solution(mesh):
    rows = P(("wide", "narrow"))
    return jax.shard_map(
        body,
        mesh=mesh,
        in_specs=(P(("wide", "narrow"), None), rows, rows, rows, P(), rows),
        out_specs=(P(), rows, P()),
        check_vma=False,
    )
```

```python
import functools
import math

import jax
import jax.numpy as jnp
from jax import lax
from jax.experimental import pallas as pl
from jax.experimental.pallas import tpu as pltpu
from jax.sharding import PartitionSpec as P

COV = 128
LEVELS = 4
COLS = COV * LEVELS
ROWS = 2048
HB = 256
SKETCH = 1024
SAMP = 4
ITERS = 4
GROUP = 8
NZ = 8
NX = 4
NY = 4
EXTRA = 8
LANES = 128

HALF_ROOT = math.sqrt(0.5)
HIGH = lax.Precision.HIGHEST
MESH = pl.DeviceIdType.MESH
F32 = jnp.float32
BF16 = jnp.bfloat16


def iota(shape, axis):
    return lax.broadcasted_iota(jnp.int32, shape, axis)


def split3(value):
    high = value.astype(BF16)
    rest = value - high.astype(F32)
    middle = rest.astype(BF16)
    low = (rest - middle.astype(F32)).astype(BF16)
    return high.astype(F32), middle.astype(F32), low.astype(F32)


def blk(index):
    return slice(index * COV, (index + 1) * COV)


def ring(offset, size):
    return min(offset, size - offset)


Z_FAR = sorted(range(1, NZ), key=lambda o: -ring(o, NZ))
FOUR_FAR = (2, 1, 3)
MIX_FAR = sorted(
    [(dx, dc) for dx in range(4) for dc in range(2) if (dx, dc) != (0, 0)],
    key=lambda o: -(ring(o[0], 4) + o[1]),
)


def gather_kernel(
    samp_hbm, cov_hbm, codes_hbm, bits_hbm, noise_hbm,
    gram_ref, square_ref, extra_ref,
    samp_ref, cov_ref, codes_ref, bits_ref, noise_ref,
    own, asked, marks, picks, lhs, sent, held, rowz, sketch,
    halves, half_in, pieces, piece_in, row_in, col_in,
    send, recv, load,
):
    loads = [
        pltpu.make_async_copy(src, dst, load.at[i])
        for i, (src, dst) in enumerate(
            [
                (samp_hbm, samp_ref), (cov_hbm, cov_ref), (codes_hbm, codes_ref),
                (bits_hbm, bits_ref), (noise_hbm, noise_ref),
            ]
        )
    ]
    for copy in loads:
        copy.start()
    wide = lax.axis_index("wide")
    z = lax.axis_index("narrow")
    core = lax.rem(wide, 2)
    q = wide // 2
    x = lax.rem(q, 4)
    y = q // 4
    member = lax.rem(wide, GROUP)
    base = wide - member
    sibling = wide + 1 - 2 * core
    mix_peers = [lax.rem(x + dx, 4) * 2 + lax.rem(core + dc, 2) for dx, dc in MIX_FAR]
    z_peers = [lax.rem(z + o, NZ) for o in Z_FAR]
    x_peers = [(y * 4 + lax.rem(x + o, 4)) * 2 + core for o in FOUR_FAR]
    y_peers = [(lax.rem(y + o, 4) * 4 + x) * 2 + core for o in FOUR_FAR]

    slots = iter(range(N_COPIES))

    def remote(src, dst, to_wide, to_z):
        slot = next(slots)
        return pltpu.make_async_remote_copy(
            src_ref=src, dst_ref=dst, send_sem=send.at[slot], recv_sem=recv.at[slot],
            device_id=(to_wide, to_z), device_id_type=MESH,
        )

    barrier = pltpu.get_barrier_semaphore()
    for peer in z_peers:
        pl.semaphore_signal(barrier, inc=1, device_id=(wide, peer), device_id_type=MESH)
    for peer in y_peers:
        pl.semaphore_signal(barrier, inc=1, device_id=(peer, z), device_id_type=MESH)
    for peer in mix_peers:
        pl.semaphore_signal(barrier, inc=1, device_id=(base + peer, z), device_id_type=MESH)

    for copy in loads[1:]:
        copy.wait()
    codes = codes_ref[...]
    flip = cov_ref[...].astype(F32).T
    masks = [(codes == level).astype(F32) for level in range(LEVELS)]
    for level in range(LEVELS):
        lhs[level * COV : (level + 1) * COV, :] = (flip * masks[level]).astype(BF16)
    parts = split3(noise_ref[...])
    shadow_rows = [part * mask for part in parts for mask in masks]
    shadow_rows = jnp.concatenate(shadow_rows + [jnp.zeros((4, ROWS), F32)], axis=0)
    normal = jnp.dot(lhs[...], cov_ref[...], preferred_element_type=F32)
    shadow = jnp.dot(shadow_rows.astype(BF16), cov_ref[...], preferred_element_type=F32)
    shadow = shadow[0:4] + shadow[4:8] + shadow[8:12]
    sub = iota((COV, COV), 0)
    lane = iota((COV, COV), 1)
    diagonals = []
    for pair in range(2):
        even = normal[2 * pair * COV : (2 * pair + 1) * COV]
        odd = normal[(2 * pair + 1) * COV : (2 * pair + 2) * COV]
        halves[pair, 0:COV, :] = jnp.where(lane >= sub, even, odd)
        diagonals.append(jnp.sum(jnp.where(lane == sub, odd, 0.0), axis=0, keepdims=True))
    extra = jnp.concatenate([shadow] + diagonals + [jnp.zeros((2, COV), F32)], axis=0)
    halves[0, COV:, :] = extra
    halves[1, COV:, :] = extra
    half = iota((8, LANES), 0) // SAMP
    for chunk in range(ROWS // LANES):
        span = slice(chunk * LANES, (chunk + 1) * LANES)
        flips = (1 - 2 * bits_ref[:, span]).astype(F32)
        for pair in range(2):
            marks[pair, chunk] = jnp.where(codes_ref[:, span] == 2 * pair + half, flips, 0.0)
    loads[0].wait()
    for k in range(8):
        own[k : k + 1, :] = jnp.full((1, LANES), samp_ref[k % SAMP], jnp.int32)
    asked[member] = own[...]
    pl.semaphore_wait(barrier, len(Z_FAR) + len(FOUR_FAR) + len(MIX_FAR))

    ask = [remote(own, asked.at[member], base + peer, z) for peer in mix_peers]
    for copy in ask:
        copy.start()

    a_core = remote(halves.at[1 - core], half_in, sibling, z)
    a_core.start()

    a_core.wait_recv()
    mine = halves[core] + half_in[...]
    for i in range(NZ):
        pieces[i] = jnp.concatenate([mine[i * 16 : (i + 1) * 16], mine[COV:]], axis=0)
    piece_in[z] = pieces[z]
    a_z = [remote(pieces.at[peer], piece_in.at[z], wide, peer) for peer in z_peers]
    for copy in a_z:
        copy.start()

    for copy in ask:
        copy.wait_recv()
    want = jnp.concatenate([asked[i] for i in range(GROUP)], axis=0)
    shape = (GROUP * 8, LANES)
    common = want & iota(shape, 1)
    common = common ^ (common >> 4)
    common = common ^ (common >> 2)
    low = common ^ (common >> 1)
    top = (want >> 7) & 1
    block = want >> 8
    even = (1 - 2 * (low & 1)).astype(F32)
    odd = even * (1 - 2 * top).astype(F32)
    for chunk in range(ROWS // LANES):
        span = slice(chunk * LANES, (chunk + 1) * LANES)
        sign = jnp.where(block == chunk // 2, odd if chunk % 2 else even, 0.0)
        for pair in range(2):
            value = sign.reshape(GROUP, 8, LANES) * marks[pair, chunk]
            picks[pair * 64 : (pair + 1) * 64, span] = value.reshape(shape).astype(BF16)
    local = jnp.dot(picks[...], cov_ref[...], preferred_element_type=F32)
    local = local * (1.0 / math.sqrt(HB))
    for i in range(GROUP):
        spots = [pair * 64 + i * 8 + SAMP * half for pair in range(2) for half in range(2)]
        sent[i] = jnp.concatenate([local[at : at + SAMP] for at in spots], axis=1).astype(BF16)
    held[member] = sent[member]
    rows = [remote(sent.at[peer], held.at[member], base + peer, z) for peer in mix_peers]
    for copy in rows:
        copy.start()

    for copy in a_z:
        copy.wait_recv()
    total = piece_in[0]
    for i in range(1, NZ):
        total = total + piece_in[i]
    row_in[x] = total
    a_x = [remote(row_in.at[x], row_in.at[x], peer, z) for peer in x_peers]
    for copy in a_x:
        copy.start()

    for copy in rows:
        copy.wait_recv()
    level_rows = [held[i].astype(F32) for i in range(GROUP)]
    for place in range(3):
        side = (1 - 2 * lax.rem(wide // (2**place), 2)).astype(F32)
        level_rows = [
            ((level_rows[i] + side * level_rows[i + 1]) * HALF_ROOT).astype(BF16).astype(F32)
            for i in range(0, len(level_rows), 2)
        ]
    rowz[z] = level_rows[0].astype(BF16)
    s_z = [remote(rowz.at[z], rowz.at[z], wide, peer) for peer in z_peers]
    for copy in s_z:
        copy.start()

    for copy in a_x:
        copy.wait_recv()
    total = row_in[0]
    for i in range(1, NX):
        total = total + row_in[i]
    col_in[y] = total
    a_y = [remote(col_in.at[y], col_in.at[y], peer, z) for peer in y_peers]
    for copy in a_y:
        copy.start()

    for copy in s_z:
        copy.wait_recv()
    stack = jnp.concatenate([rowz[i].astype(F32) for i in range(NZ)], axis=0).astype(BF16)
    sketch[core, 0, y, x] = stack[:16]
    sketch[core, 1, x, y] = stack[16:]
    first = sketch.at[core, 0, y, x]
    second = sketch.at[core, 1, x, y]
    s_first = [remote(first, first, peer, z) for peer in x_peers]
    s_second = [remote(second, second, peer, z) for peer in y_peers]
    for one, two in zip(s_first, s_second):
        one.start()
        two.start()
    s_line = [[] for _ in FOUR_FAR]
    s_other = [[] for _ in FOUR_FAR]

    def along(x_from, y_from):
        line = sketch.at[core, 0, y, x_from]
        other = sketch.at[core, 1, x, y_from]
        for i in range(len(FOUR_FAR)):
            s_line[i].append(remote(line, line, y_peers[i], z))
            s_other[i].append(remote(other, other, x_peers[i], z))
            s_line[i][-1].start()
            s_other[i][-1].start()

    along(x, y)

    for copy in a_y:
        copy.wait_recv()
    total = col_in[0]
    for i in range(1, NY):
        total = total + col_in[i]
    extra_ref[...] = total[16:]
    square_ref[core, z] = total[:16]
    mine = square_ref.at[core, z]
    a_out = [remote(mine, mine, wide, peer) for peer in z_peers]
    for copy in a_out:
        copy.start()

    for i in (2, 1, 0):
        s_first[i].wait_recv()
        s_second[i].wait_recv()
        along(lax.rem(x - FOUR_FAR[i] + 4, 4), lax.rem(y - FOUR_FAR[i] + 4, 4))
    line = sketch.at[core, 0, y]
    other = sketch.at[core, 1, x]
    s_core = [remote(line, line, sibling, z), remote(other, other, sibling, z)]
    for copy in s_core:
        copy.start()

    def onward(index):
        for copy in s_line[index]:
            copy.wait_recv()
        passed = sketch.at[core, 0, lax.rem(y - FOUR_FAR[index] + 4, 4)]
        copy = remote(passed, passed, sibling, z)
        copy.start()
        s_core.append(copy)
        for copy in s_other[index]:
            copy.wait_recv()
        passed = sketch.at[core, 1, lax.rem(x - FOUR_FAR[index] + 4, 4)]
        copy = remote(passed, passed, sibling, z)
        copy.start()
        s_core.append(copy)

    onward(1)
    onward(2)
    for copy in a_out:
        copy.wait_recv()
    a_last = remote(square_ref.at[core], square_ref.at[core], sibling, z)
    a_last.start()
    onward(0)

    def gram_of(source, k):
        rows = sketch[source].reshape(SKETCH // 2, COLS)
        return lax.dot_general(
            rows[:, blk(k)], rows[:, k * COV :], (((0,), (0,)), ((), ())),
            preferred_element_type=F32,
        )

    for k in range(LEVELS):
        gram_ref[k, :, k * COV :] = gram_of(core, k)
    a_last.wait_recv()
    for copy in s_core:
        copy.wait_recv()
    for k in range(LEVELS):
        gram_ref[k, :, k * COV :] = gram_ref[k, :, k * COV :] + gram_of(1 - core, k)
    sums = [a_core] + a_z + a_x + a_y + a_out + [a_last]
    lines = [copy for group in s_line + s_other for copy in group]
    for copy in ask + rows + s_z + s_first + s_second + lines + s_core + sums:
        copy.wait_send()


N_COPIES = 7 + 1 + 7 + 7 + 7 + 3 + 6 + 3 + 24 + 8 + 7 + 1


def gather(samples, covariates, codes, bits, noise):
    vmem = pl.BlockSpec(memory_space=pltpu.VMEM)
    hbm = pl.BlockSpec(memory_space=pltpu.HBM)
    return pl.pallas_call(
        gather_kernel,
        out_shape=(
            jax.ShapeDtypeStruct((LEVELS, COV, COLS), F32),
            jax.ShapeDtypeStruct((2, NZ, 16, COV), F32),
            jax.ShapeDtypeStruct((EXTRA, COV), F32),
        ),
        in_specs=[hbm] * 5,
        out_specs=(vmem, vmem, vmem),
        scratch_shapes=[
            pltpu.SMEM((SAMP,), jnp.int32),
            pltpu.VMEM((ROWS, COV), BF16),
            pltpu.VMEM((1, ROWS), jnp.int32),
            pltpu.VMEM((1, ROWS), jnp.int32),
            pltpu.VMEM((1, ROWS), F32),
            pltpu.VMEM((8, LANES), jnp.int32),
            pltpu.VMEM((GROUP, 8, LANES), jnp.int32),
            pltpu.VMEM((2, ROWS // LANES, 8, LANES), F32),
            pltpu.VMEM((2 * 64, ROWS), BF16),
            pltpu.VMEM((COLS, ROWS), BF16),
            pltpu.VMEM((GROUP, SAMP, COLS), BF16),
            pltpu.VMEM((GROUP, SAMP, COLS), BF16),
            pltpu.VMEM((NZ, SAMP, COLS), BF16),
            pltpu.VMEM((2, 2, NY, NX, 16, COLS), BF16),
            pltpu.VMEM((2, COV + EXTRA, COV), F32),
            pltpu.VMEM((COV + EXTRA, COV), F32),
            pltpu.VMEM((NZ, 16 + EXTRA, COV), F32),
            pltpu.VMEM((NZ, 16 + EXTRA, COV), F32),
            pltpu.VMEM((NX, 16 + EXTRA, COV), F32),
            pltpu.VMEM((NY, 16 + EXTRA, COV), F32),
            pltpu.SemaphoreType.DMA((N_COPIES,)),
            pltpu.SemaphoreType.DMA((N_COPIES,)),
            pltpu.SemaphoreType.DMA((5,)),
        ],
        compiler_params=pltpu.CompilerParams(
            collective_id=0, has_side_effects=True, vmem_limit_bytes=40 << 20
        ),
        name="gather_sketch",
    )(samples, covariates, codes, bits, noise)


def column(value, index):
    return jnp.broadcast_to(value[:, index : index + 1], value.shape)


def six(value, order, axis):
    parts = split3(value)
    return jnp.concatenate([parts[i] for i in order], axis=axis).astype(BF16)


def product6(left, right, turned=False):
    axis = 0 if turned else 1
    return lax.dot_general(
        six(left, (0, 0, 0, 1, 1, 2), axis), six(right, (0, 1, 2, 0, 1, 0), 0),
        (((axis,), (0,)), ((), ())), preferred_element_type=F32,
    )


AHEAD = 4
PANEL = 8
SLOTS = 2 * PANEL + 1


def invert_factor(matrix, slots):
    count = COV // PANEL
    shape = (PANEL, COV)
    rows = [matrix[PANEL * t : PANEL * (t + 1), :] for t in range(count)]
    sub = iota(shape, 0)
    lane = iota(shape, 1)

    def columns(t, first):
        return [column(rows[t], first + i) for i in range(PANEL)]

    def spread(slot, index):
        return slots[slot, pl.ds(index, PANEL, stride=0), :]

    pivot = columns(0, 0)
    for p in range(count):
        base = (p % 2) * SLOTS
        first = PANEL * p
        panel = (lane >= first) & (lane < first + PANEL)
        near = range(p + 1, min(p + 1 + AHEAD, count))
        far = range(min(p + 1 + AHEAD, count), count)
        own = {t: columns(t, first) for t in near}
        after = columns(p + 1, first + PANEL) if p + 1 < count else None
        for c in range(PANEL):
            slots[base + c] = pivot[c]
        left = [[spread(base + c, a) for c in range(a + 1)] for a in range(PANEL)]
        rows[p] = jnp.where(panel, jnp.where(lane == first + sub, 1.0, 0.0), rows[p])
        slots[base + PANEL] = rows[p]
        start = [spread(base + PANEL, i) for i in range(PANEL)]
        root = []
        low = [[None] * PANEL for _ in range(PANEL)]
        for i in range(PANEL):
            root.append(lax.rsqrt(left[i][i]))
            for a in range(i + 1, PANEL):
                low[a][i] = left[a][i] * root[i]
            for a in range(i + 1, PANEL):
                for c in range(i + 1, a + 1):
                    left[a][c] = left[a][c] - low[a][i] * low[c][i]

        def multipliers(t):
            scales = []
            for i in range(PANEL):
                scale = own[t][i]
                for k in range(i):
                    scale = scale - scales[k] * low[i][k]
                scales.append(scale * root[i])
            return scales

        scales = {}
        if after:
            scales[p + 1] = multipliers(p + 1)
            for i, scale in enumerate(scales[p + 1]):
                slot = base + PANEL + 1 + i
                slots[slot] = scale
                for c in range(PANEL):
                    after[c] = after[c] - scale * spread(slot, c)
            pivot = after
        row = []
        for i in range(PANEL):
            value = start[i]
            for k in range(i):
                value = value - low[i][k] * row[k]
            row.append(value * root[i])
        value = row[PANEL - 1]
        for i in range(PANEL - 1):
            value = jnp.where(sub == i, row[i], value)
        rows[p] = value
        if len(far):
            change = product6(value, value, turned=True)
        for t in near:
            if t not in scales:
                scales[t] = multipliers(t)
            value = jnp.where(panel, 0.0, rows[t])
            for scale, one in zip(scales[t], row):
                value = value - scale * one
            rows[t] = value
        for t in far:
            rows[t] = jnp.where(panel, 0.0, rows[t]) - change[PANEL * t : PANEL * (t + 1), :]
    for p in range(count):
        rows[p] = jnp.where(lane <= PANEL * p + sub, rows[p], 0.0)
    return jnp.concatenate(rows, axis=0)


def solve_kernel(
    given, square_ref, extra_ref, effects_hbm, cov_hbm, codes_hbm, noise_hbm,
    coef_ref, resid_ref, factor_hbm, gram, inverse,
    factor_ref, effects_ref, cov_ref, codes_ref, noise_ref, slots, load, store,
):
    loads = [
        pltpu.make_async_copy(src, dst, load.at[i])
        for i, (src, dst) in enumerate(
            [
                (effects_hbm, effects_ref), (cov_hbm, cov_ref), (codes_hbm, codes_ref),
                (noise_hbm, noise_ref),
            ]
        )
    ]
    for copy in loads:
        copy.start()
    stores = []
    n = LEVELS
    sub = iota((COV, COV), 0)
    lane = iota((COV, COV), 1)
    scale = math.sqrt(LEVELS / SKETCH)
    matrix = given[0, :, blk(0)]
    for k in range(n):
        held = gram if k else given
        current = matrix
        corner = invert_factor(current, slots)
        inverse[k, :, blk(k)] = corner
        head = None
        if k + 1 < n:
            head = product6(corner, held[k, :, blk(k + 1)])
            matrix = held[k + 1, :, blk(k + 1)] - product6(head, head, turned=True)
        if k:
            inverse[k, :, : k * COV] = product6(corner, gram[k, :, : k * COV])
            factor_ref[blk(k), : k * COV] = jnp.zeros((COV, k * COV), F32)
        own = product6(corner, current)
        factor_ref[blk(k), blk(k)] = jnp.where(lane >= sub, own, 0.0) * scale
        upper = {k + 1: head}
        if k + 1 < n:
            factor_ref[blk(k), blk(k + 1)] = head * scale
        if k + 2 < n:
            rest = product6(corner, held[k, :, (k + 2) * COV :])
            factor_ref[blk(k), (k + 2) * COV :] = rest * scale
            for i in range(k + 2, n):
                upper[i] = rest[:, blk(i - k - 2)]
        part = pltpu.make_async_copy(factor_ref.at[blk(k)], factor_hbm.at[blk(k)], store.at[k])
        part.start()
        stores.append(part)
        for i in range(k + 1, n):
            for j in range(i, n):
                if j > k + 1:
                    change = product6(upper[i], upper[j], turned=True)
                    gram[i, :, blk(j)] = held[i, :, blk(j)] - change
            change = product6(upper[i], inverse[k, :, : (k + 1) * COV], turned=True)
            if k:
                gram[i, :, : k * COV] = gram[i, :, : k * COV] - change[:, : k * COV]
            gram[i, :, blk(k)] = -change[:, blk(k)]

    normal = []
    for pair in range(2):
        square = square_ref[pair]
        turned = square.T
        diagonal = extra_ref[4 + pair : 5 + pair, :]
        normal.append(jnp.where(lane >= sub, square, turned))
        normal.append(jnp.where(lane < sub, square, jnp.where(lane > sub, turned, diagonal)))

    def apply_normal(rows):
        out = []
        for level in range(n):
            column = jnp.sum(normal[level] * rows[level], axis=1, keepdims=True)
            out.append(jnp.sum(jnp.where(lane == sub, column, 0.0), axis=0, keepdims=True))
        return out

    def forward(rows):
        out = []
        for k in range(n):
            acc = inverse[k, :, blk(0)] * rows[0]
            for c in range(1, k + 1):
                acc = acc + inverse[k, :, blk(c)] * rows[c]
            out.append(jnp.sum(acc, axis=1, keepdims=True))
        return out

    def backward(columns):
        out = []
        for c in range(n):
            acc = inverse[c, :, blk(c)] * columns[c]
            for k in range(c + 1, n):
                acc = acc + inverse[k, :, blk(c)] * columns[k]
            out.append(jnp.sum(acc, axis=0, keepdims=True))
        return out

    def dot(left, right, axis):
        acc = left[0] * right[0]
        for a, b in zip(left[1:], right[1:]):
            acc = acc + a * b
        return jnp.sum(acc, axis=axis, keepdims=True)

    for copy in loads:
        copy.wait()
    effects = [effects_ref[:, blk(level)] for level in range(n)]
    gradient = [
        image + extra_ref[level : level + 1, :] for level, image in enumerate(apply_normal(effects))
    ]
    steer = forward(gradient)
    gamma = dot(steer, steer, 0)
    direction = backward(steer)
    solved = [jnp.zeros((1, COV), F32)] * n
    for step in range(ITERS):
        image = apply_normal(direction)
        alpha = gamma / dot(direction, image, 1)
        solved = [a + alpha * b for a, b in zip(solved, direction)]
        if step + 1 < ITERS:
            gradient = [a - alpha * b for a, b in zip(gradient, image)]
            steer = forward(gradient)
            gamma_new = dot(steer, steer, 0)
            ratio = gamma_new / gamma
            direction = [a + ratio * b for a, b in zip(backward(steer), direction)]
            gamma = gamma_new
    left = []
    for level in range(n):
        coef_ref[:, blk(level)] = solved[level]
        left.append(effects[level] - solved[level])
    parts = split3(jnp.concatenate(left, axis=0))
    weights = jnp.concatenate(list(parts) + [jnp.zeros((4, COV), F32)], axis=0).astype(BF16)
    values = lax.dot_general(
        weights, cov_ref[...], (((1,), (1,)), ((), ())), preferred_element_type=F32
    )
    codes = codes_ref[...]
    resid = noise_ref[...]
    for level in range(n):
        value = values[level : level + 1] + values[4 + level : 5 + level] + values[8 + level : 9 + level]
        resid = resid + jnp.where(codes == level, value, 0.0)
    resid_ref[...] = resid
    for copy in stores:
        copy.wait()


def solve(gram, square, extra, effects, covariates, codes, noise):
    vmem = pl.BlockSpec(memory_space=pltpu.VMEM)
    hbm = pl.BlockSpec(memory_space=pltpu.HBM)
    return pl.pallas_call(
        solve_kernel,
        out_shape=(
            jax.ShapeDtypeStruct((1, COLS), F32),
            jax.ShapeDtypeStruct((1, ROWS), F32),
            jax.ShapeDtypeStruct((COLS, COLS), F32),
        ),
        in_specs=[vmem] * 3 + [hbm] * 4,
        out_specs=(vmem, vmem, hbm),
        scratch_shapes=[
            pltpu.VMEM((LEVELS, COV, COLS), F32),
            pltpu.VMEM((LEVELS, COV, COLS), F32),
            pltpu.VMEM((COLS, COLS), F32),
            pltpu.VMEM((1, COLS), F32),
            pltpu.VMEM((ROWS, COV), BF16),
            pltpu.VMEM((1, ROWS), jnp.int32),
            pltpu.VMEM((1, ROWS), F32),
            pltpu.VMEM((2 * SLOTS, PANEL, COV), F32),
            pltpu.SemaphoreType.DMA((4,)),
            pltpu.SemaphoreType.DMA((LEVELS,)),
        ],
        compiler_params=pltpu.CompilerParams(vmem_limit_bytes=40 << 20),
        name="solve",
    )(gram, square, extra, effects, covariates, codes, noise)


def body(covariates, level_codes, sign_bits, sample_rows, effects, noise):
    def fixed(value):
        return pltpu.with_memory_space_constraint(value, pltpu.HBM)

    covariates = fixed(covariates)
    codes = fixed(level_codes.reshape(1, ROWS))
    noise = fixed(noise.reshape(1, ROWS))
    gram, square, extra = gather(
        fixed(sample_rows), covariates, codes, fixed(sign_bits.reshape(1, ROWS)), noise
    )
    coef, resid, factor = solve(
        gram, square.reshape(2, COV, COV), extra,
        fixed(effects.reshape(1, COLS)), covariates, codes, noise,
    )
    return coef.reshape(COLS), resid.reshape(ROWS), factor


def solution(mesh):
    rows = P(("wide", "narrow"))
    return jax.shard_map(
        body,
        mesh=mesh,
        in_specs=(P(("wide", "narrow"), None), rows, rows, rows, P(), rows),
        out_specs=(P(), rows, P()),
        check_vma=False,
    )
```
